128 devices in a mesh: dp: 32 (over x, z, core), tensor: 4 (over y).
Axes of the slice: x: 4, y: 4, z: 4, core: 2. Of those that a mesh axis runs over, the one named last changes fastest.
Arguments:
- hidden: bfloat16 [32768, 2560], P('dp', 'tensor'), may hold values from -6 to 6
- out_grad: bfloat16 [32768, 2560], P('dp', 'tensor'), may hold values from -6 to 6
- memory: bfloat16 [32768, 1280], P('dp'), may hold values from -6 to 6
- w_key: bfloat16 [1280, 2560], P(None, 'tensor'), may hold values from -0.15625 to 0.15625
- w_value: bfloat16 [1280, 2560], P(None, 'tensor'), may hold values from -0.15625 to 0.15625
- row_owner: int32 [32768, 8], P('dp'), may hold values from 0 to 127, all different within a row; in each aligned block of 256 rows (0 to 255, 256 to 511, ...) at most 32 rows name the same one
- row_slot: int32 [32768, 8], P('dp'), may hold values from 0 to 511
- mem_table: float32 [65536, 160], P(('dp', 'tensor')), may hold values from -6 to 6
- adagrad_sum: float32 [65536, 160], P(('dp', 'tensor')), may hold values from 0.05 to 2
Outputs:
- hidden_grad: bfloat16 [32768, 2560], P('dp', 'tensor')
- key_weight_grad: float32 [1280, 2560], P('dp', 'tensor')
- value_weight_grad: float32 [1280, 2560], P('dp', 'tensor')
- new_table: float32 [65536, 160], P(('dp', 'tensor'))
- new_sum: float32 [65536, 160], P(('dp', 'tensor'))
The draws below stay inside these ranges and needn't reach their ends.
Inputs may be any that keep to these rules, and one draw needn't show every extreme that they name: `row_owner`: each token's 8 owners are distinct. Within a dp shard, take the tokens in order in aligned blocks of 256: in each block no owner is named more than 32 times, a bound that some owner reaches in some or all blocks. `row_slot`: A few row indices are retrieved very often.
All inputs are finite; a program needn't handle non-finite values.
Results may differ from the reference program's by a relative error of at most 0.0034.
Values sent between devices are 32-bit elements; how exact they have to be, the bound alone decides.
No kernel may reach another device: no remote copies, remote signals or barrier semaphores. Data moves between devices by JAX's collectives and lax.ppermute only.
A program may use at most 128 MiB of HBM per device.

```python
import math
import jax
import jax.numpy as jnp
import numpy as np
from jax import lax

D = 2560
ME = 1280
H = 8
TOK_DEV = 1024
R_DEV = 512
CAP = 32
EH = 160
TOKENS = 32768
ROWS = 65536
N_DP = 32
N_TENSOR = 4


def touch_ends(entries, stream_key, least, high):
    extent = entries.shape
    index_at = [jax.random.randint(jax.random.fold_in(stream_key, axis), (), 0, extent[axis]) for axis in range(len(extent))]
    entries = entries.at[tuple(index_at)].set(least)
    longest = extent.index(max(extent))
    index_at[longest] = (index_at[longest] + 1) % extent[longest]
    return entries.at[tuple(index_at)].set(high)


def block_scale(rng, dims, pieces, smallest, high):
    gain = 1.0
    for position, parts in pieces:
        steps = jax.random.uniform(jax.random.fold_in(jax.random.fold_in(rng, 6), position), (parts,), jnp.float32, smallest / len(pieces), high / len(pieces))
        gain = gain * jnp.repeat(jnp.exp(steps), dims[position] // parts).reshape((-1,) + (1,) * (len(dims) - 1 - position))
    return gain


def cumulative_ranks(number_of, lean):
    loads = [(1 << 20) // math.isqrt(rank ** lean) + 1 for rank in range(1, number_of + 1)]
    scale = 1 + sum(loads) // (1 << 30)
    return np.cumsum(np.array([max(1, weight // scale) for weight in loads]))


def ranked_ids(own_key, shape, amount, skew):
    table = cumulative_ranks(amount, skew)
    ticket = jax.random.randint(jax.random.fold_in(own_key, 1), shape, 0, int(table[amount - 1]))
    grade = jnp.searchsorted(jnp.asarray(table, jnp.int32), ticket, side="right")
    return jax.random.permutation(jax.random.fold_in(own_key, 2), amount)[grade].astype(jnp.int32)


def assign_block(key, own, number, rows, number_of, top, reach, skew):
    sequence = jax.random.permutation(key, number_of)
    crowded, ordinary = portions_of(number_of, rows * top, reach, skew, True), portions_of(number_of, rows * top, reach, skew, False)
    places = jnp.arange(number_of)

    def named(tallies, rotation):
        used = int((tallies > 0).sum())
        fixed = max(1, used // 4)
        passed = fixed + (places - fixed + rotation * (used - fixed)) % max(1, number_of - fixed)
        return jnp.zeros((number_of,), jnp.int32).at[sequence[jnp.where(places < fixed, places, passed)]].set(jnp.asarray(tallies, jnp.int32))

    tallies = jnp.where(number % 4 == 0, named(crowded, number // 4), named(ordinary, number - number // 4 - 1))
    mixed = jax.random.permutation(jax.random.fold_in(own, 3), number_of)
    donor, receiver = mixed[0:number_of // 2 * 2:2], mixed[1:number_of // 2 * 2:2]
    margin = jnp.minimum(tallies[donor] - 1, reach - tallies[receiver]) // 2
    margin = jnp.where((donor == sequence[0]) | (receiver == sequence[0]) | (tallies[receiver] == 0), 0, jnp.maximum(margin, 0))
    passed = jax.random.randint(jax.random.fold_in(own, 4), (number_of // 2,), 0, 1 << 20) % (margin + 1)
    tallies = tallies.at[donor].add(-passed).at[receiver].add(passed)
    members = jnp.searchsorted(jnp.cumsum(tallies), jnp.arange(rows * top), side="right").astype(jnp.int32)
    table = members.reshape(top, rows).T
    table = table[jax.random.permutation(jax.random.fold_in(own, 1), rows)]
    rotation = jax.random.randint(jax.random.fold_in(own, 2), (rows, 1), 0, top)
    return jnp.take_along_axis(table, (jnp.arange(top)[None, :] + rotation) % top, axis=1)


def portions_of(number_of, total, bound, slope, full):
    portions = [(1 << 20) // math.isqrt(grade ** slope) + 1 for grade in range(1, number_of + 1)]
    largest = bound if full else min(bound, max(-(-total // number_of), total * portions[0] // sum(portions)))
    least = 1 if total - largest >= number_of - 1 else 0
    given, spare = [largest] + [least] * (number_of - 1), total - largest - least * (number_of - 1)
    while spare > 0:
        candidates = [i for i in range(1, number_of) if given[i] < largest] or [i for i in range(1, number_of) if given[i] < bound]
        mass, remaining = sum([portions[i] for i in candidates]), spare
        for i in candidates:
            extra = min(bound - given[i], max(1, remaining * portions[i] // mass), spare)
            given[i] = given[i] + extra
            spare = spare - extra
    return np.array(given)


def noise(key, extent, deviation, reach, shards=(), dtype=jnp.bfloat16):
    values = jax.random.normal(key, extent, jnp.float32) * deviation
    if len(shards) > 0:
        values = block_scale(key, extent, shards, -0.22, 0.18) * values
    return jnp.clip(values, min=-reach, max=reach).astype(dtype)


def setup_inputs(seed: int = 0) -> dict:
    streams_of = jax.random.split(jax.random.key(seed), 10)
    hidden = noise(streams_of[0], (TOKENS, D), 1.0, 6.0, ((0, 32), (1, 4)))
    out_grad = noise(streams_of[1], (TOKENS, D), 1.0, 6.0, ((0, 32), (1, 4)))
    memory = noise(streams_of[2], (TOKENS, ME), 1.0, 6.0, ((0, 32),))
    w_key = noise(streams_of[3], (ME, D), ME ** -0.5, 0.15625, ((1, 4),))
    w_value = noise(streams_of[4], (ME, D), ME ** -0.5, 0.15625, ((1, 4),))
    row_owner_keys = jax.random.split(jax.random.fold_in(streams_of[5], 1), TOKENS // (TOK_DEV // N_TENSOR))
    row_owner_turns = jax.random.permutation(jax.random.fold_in(streams_of[5], 3), TOKENS // (TOK_DEV // N_TENSOR))
    row_owner = jax.vmap(lambda own, number: assign_block(jax.random.fold_in(streams_of[5], 2), own, number, TOK_DEV // N_TENSOR, N_DP * N_TENSOR, H, CAP, 2))(row_owner_keys, row_owner_turns).reshape((TOKENS, H))
    row_slot = touch_ends(ranked_ids(streams_of[6], (TOKENS, H), R_DEV, 2), jax.random.fold_in(streams_of[6], 3), 0, R_DEV - 1).astype(jnp.int32)
    mem_table = noise(streams_of[7], (ROWS, EH), 1.0, 6.0, ((0, 128),), jnp.float32)
    adagrad_sum = jnp.clip(jnp.exp(math.log(2.0) - 3.6888794 * jax.random.uniform(streams_of[8], (ROWS, EH), jnp.float32) ** block_scale(streams_of[8], (ROWS, EH), ((0, 128),), -0.2, 0.2)), 0.05, 2.0)
    return {"hidden": hidden, "out_grad": out_grad, "memory": memory, "w_key": w_key, "w_value": w_value, "row_owner": row_owner, "row_slot": row_slot, "mem_table": mem_table, "adagrad_sum": adagrad_sum}


LEARN_RATE = 0.5
EPSILON = 1e-06

def reference(hidden, out_grad, memory, w_key, w_value, row_owner, row_slot, mem_table, adagrad_sum):
    scale_root = jnp.sqrt(jnp.asarray(D, jnp.float32))
    proj_key = jnp.dot(memory, w_key, preferred_element_type=jnp.float32)
    proj_value = jnp.dot(memory, w_value, preferred_element_type=jnp.float32)
    scores = lax.optimization_barrier(jnp.sum(hidden.astype(jnp.float32) * proj_key, axis=1)) / scale_root
    gate_value = jax.nn.sigmoid(scores)
    gate_grad = lax.optimization_barrier(jnp.sum(out_grad.astype(jnp.float32) * proj_value, axis=1))
    score_grad = gate_grad * gate_value * (1.0 - gate_value) / scale_root
    value_grad = (gate_value[:, None] * out_grad.astype(jnp.float32)).astype(jnp.bfloat16)
    key_grad = (score_grad[:, None] * hidden.astype(jnp.float32)).astype(jnp.bfloat16)
    hidden_grad = (score_grad[:, None] * proj_key).astype(jnp.bfloat16)
    over_tokens = (((0,), (0,)), ((), ()))
    key_weight_grad = lax.dot_general(memory, key_grad, over_tokens, preferred_element_type=jnp.float32)
    value_weight_grad = lax.dot_general(memory, value_grad, over_tokens, preferred_element_type=jnp.float32)
    over_features = (((1,), (1,)), ((), ()))
    memory_grad = lax.dot_general(value_grad, w_value, over_features, preferred_element_type=jnp.float32)
    memory_grad = memory_grad + lax.dot_general(key_grad, w_key, over_features, preferred_element_type=jnp.float32)
    row_index = (row_owner * R_DEV + row_slot).reshape(-1).astype(jnp.int32)
    row_grads = memory_grad.reshape(-1, ME // H)
    row_sum = jax.ops.segment_sum(row_grads, row_index, num_segments=R_DEV * N_DP * N_TENSOR)
    new_sum = adagrad_sum + row_sum * row_sum
    new_table = mem_table - LEARN_RATE * row_sum / (jnp.sqrt(new_sum) + EPSILON)
    return (hidden_grad, key_weight_grad, value_weight_grad, new_table, new_sum)
```

```python
import functools

import jax
import jax.numpy as jnp
from jax import lax
from jax.experimental import pallas as pl
from jax.experimental.pallas import tpu as pltpu
from jax.sharding import PartitionSpec as P

D = 2560
HEADS = 8
EH = 160
MAIN = 128
TAIL = EH - MAIN
CAP = 32
GROUP = CAP // 4
CHUNK = CAP + GROUP + 1
LEARN_RATE = 0.5
EPSILON = 1e-06
F32 = jnp.float32
BF16 = jnp.bfloat16
OVER_ROWS = (((0,), (0,)), ((), ()))
OVER_LANES = (((1,), (1,)), ((), ()))


def params(mib):
    return pltpu.CompilerParams(vmem_limit_bytes=mib << 20)


def cost(flops, moved):
    return pl.CostEstimate(flops=flops, bytes_accessed=moved, transcendentals=0)


def row_sums(x):
    lanes = x[:, :128]
    for at in range(128, x.shape[1], 128):
        lanes = lanes + x[:, at : at + 128]
    return jnp.sum(lanes.T, axis=0, keepdims=True)


def as_columns(row, width):
    column = jnp.broadcast_to(row, (128, row.shape[1])).T
    return jnp.concatenate([column] * (width // 128), axis=1)


def ranks_kernel(at_ref, owners_ref, slots_ref, ranks_ref, sent_ref):
    count = owners_ref.shape[1]
    owners = owners_ref[...]
    slot_plus = slots_ref[...] + 1
    ids = lax.broadcasted_iota(jnp.int32, (128, count), 0)
    hits = jnp.zeros((128, count), F32)
    for h in range(HEADS):
        hits = hits + jnp.where(owners[h : h + 1] == ids, 1.0, 0.0)
    earlier = lax.broadcasted_iota(jnp.int32, (count, count), 0) < lax.broadcasted_iota(
        jnp.int32, (count, count), 1
    )
    before = jnp.dot(
        hits.astype(BF16), jnp.where(earlier, 1.0, 0.0).astype(BF16), preferred_element_type=F32
    )
    high = jnp.zeros((128, 128), F32)
    low = jnp.zeros((128, 128), F32)
    for h in range(HEADS):
        match = owners[h : h + 1] == ids
        rank = jnp.sum(jnp.where(match, before, 0.0), axis=0, keepdims=True).astype(jnp.int32)
        ranks_ref[h : h + 1, :] = rank
        place = jnp.where(rank == ids, 1.0, 0.0).astype(BF16)
        slot = slot_plus[h : h + 1]
        upper = jnp.where(match, (slot // 16).astype(F32), 0.0).astype(BF16)
        lower = jnp.where(match, (slot % 16).astype(F32), 0.0).astype(BF16)
        high = high + lax.dot_general(upper, place, OVER_LANES, preferred_element_type=F32)
        low = low + lax.dot_general(lower, place, OVER_LANES, preferred_element_type=F32)
    sent_ref[...] = 16.0 * high + low


def forward_kernel(memory_ref, hidden_ref, grad_ref, wk_ref, wv_ref, key_ref, part_ref):
    memory = memory_ref[...]
    proj_key = jnp.dot(memory, wk_ref[...], preferred_element_type=F32)
    key_ref[...] = proj_key
    part_ref[0:1, :] = row_sums(hidden_ref[...].astype(F32) * proj_key)
    proj_value = jnp.dot(memory, wv_ref[...], preferred_element_type=F32)
    part_ref[1:2, :] = row_sums(grad_ref[...].astype(F32) * proj_value)


def gate_kernel(p0, p1, p2, p3, hidden_ref, grad_ref, key_ref, both_ref, hidden_grad_ref):
    width = hidden_ref.shape[1]
    total = (p0[...] + p1[...]) + (p2[...] + p3[...])
    root = jnp.sqrt(jnp.full((1, 1), D, F32))
    gate = jax.nn.sigmoid(total[0:1] / root)
    score = total[1:2] * gate * (1.0 - gate) / root
    gates = as_columns(gate, width)
    scores = as_columns(score, width)
    both_ref[:, :width] = (scores * hidden_ref[...].astype(F32)).astype(BF16)
    both_ref[:, width:] = (gates * grad_ref[...].astype(F32)).astype(BF16)
    hidden_grad_ref[...] = (scores * key_ref[...]).astype(BF16)


def memory_grad_kernel(at_ref, left_ref, right_ref, wk_ref, wv_ref, out_left, out_right):
    width = wk_ref.shape[1]
    half = HEADS // 2

    def product(both, first, rows):
        return lax.dot_general(
            both[:, :width], wk_ref[first : first + rows, :], OVER_LANES, preferred_element_type=F32
        ) + lax.dot_general(
            both[:, width:], wv_ref[first : first + rows, :], OVER_LANES, preferred_element_type=F32
        )

    for both_ref, out_ref, base in ((left_ref, out_left, 0), (right_ref, out_right, half)):
        both = both_ref[...]
        for h in range(half):
            head = product(both, (base + h) * EH, EH)
            out_ref[0, :, h * MAIN : (h + 1) * MAIN] = head[:, :MAIN]
            out_ref[0, :, half * MAIN + h * TAIL : half * MAIN + (h + 1) * TAIL] = head[:, MAIN:]


def weight_grad_kernel(memory_ref, both_ref, out_ref):
    out_ref[...] = lax.dot_general(
        memory_ref[...], both_ref[...], OVER_ROWS, preferred_element_type=F32
    )


def pack_kernel(left_ref, right_ref, owners_ref, ranks_ref, sent_ref, out_ref, select, rows, tails):
    j = pl.program_id(0)
    count = owners_ref.shape[1]
    half = HEADS // 2
    lane_group = lax.broadcasted_iota(jnp.int32, (count, 128), 1) // TAIL
    ids = lax.broadcasted_iota(jnp.int32, (128, count), 0)
    for h in range(HEADS):
        source = (left_ref, right_ref)[h // half]
        at = h % half

        @pl.when(j == 0)
        def _():
            main = source[:, at * MAIN : (at + 1) * MAIN]
            top = main.astype(BF16)
            rows[h * count : (h + 1) * count, :MAIN] = top
            rows[h * count : (h + 1) * count, 256 : 256 + MAIN] = (main - top.astype(F32)).astype(
                BF16
            )

        tail = source[:, half * MAIN : half * MAIN + 128]
        tail = pltpu.roll(tail, (j - at + 4) % 4 * TAIL, 1)
        tail = jnp.where(lane_group == j, tail, 0.0)
        top = tail.astype(BF16)
        rows[h * count : (h + 1) * count, MAIN:256] = top
        rows[h * count : (h + 1) * count, 256 + MAIN :] = (tail - top.astype(F32)).astype(BF16)
        match = jnp.where(owners_ref[h : h + 1, :] == ids, 1.0, 0.0).astype(BF16)
        rank = ranks_ref[h : h + 1, :]
        for k in range(GROUP):
            here = jnp.where(rank == j * GROUP + k, 1.0, 0.0)
            here = jnp.broadcast_to(here, (128, count)).astype(BF16)
            select[k * 128 : (k + 1) * 128, h * count : (h + 1) * count] = match * here
    found = jnp.dot(select[...], rows[...], preferred_element_type=F32)
    found = found[:, :256] + found[:, 256:]

    @pl.when(j == 0)
    def _():
        tails[...] = found[:, MAIN:]

    @pl.when(j > 0)
    def _():
        tails[...] += found[:, MAIN:]

    for k in range(GROUP):
        out_ref[pl.ds(j * GROUP + k, 128, stride=CHUNK), :] = found[k * 128 : (k + 1) * 128, :MAIN]

    @pl.when(j == pl.num_programs(0) - 1)
    def _():
        for k in range(GROUP):
            out_ref[pl.ds(CAP + k, 128, stride=CHUNK), :] = tails[k * 128 : (k + 1) * 128, :]
        out_ref[pl.ds(CAP + GROUP, 128, stride=CHUNK), :] = sent_ref[...]


def update_kernel(got_ref, table_ref, sums_ref, new_table_ref, new_sum_ref, values, select):
    owned = table_ref.shape[1]
    slots = got_ref[pl.ds(CAP + GROUP, 128, stride=CHUNK), :]
    ids = (lax.broadcasted_iota(jnp.int32, (128, owned), 1) + 1).astype(F32)
    for k in range(CAP):
        at = slice(k * 128, (k + 1) * 128)
        select[at, :] = jnp.where(slots[:, k : k + 1] == ids, 1.0, 0.0).astype(BF16)
        main = got_ref[pl.ds(k, 128, stride=CHUNK), :].T
        top = main.astype(BF16)
        values[:MAIN, at] = top
        values[EH : EH + MAIN, at] = (main - top.astype(F32)).astype(BF16)
    for k in range(GROUP):
        tail = got_ref[pl.ds(CAP + k, 128, stride=CHUNK), :].T
        top = tail.astype(BF16)
        rest = (tail - top.astype(F32)).astype(BF16)
        for j in range(4):
            at = slice((j * GROUP + k) * 128, (j * GROUP + k + 1) * 128)
            values[MAIN:EH, at] = top[j * TAIL : (j + 1) * TAIL]
            values[EH + MAIN :, at] = rest[j * TAIL : (j + 1) * TAIL]
    both = jnp.dot(values[...], select[...], preferred_element_type=F32)
    row_sum = both[:EH] + both[EH:]
    new_sum = sums_ref[...] + row_sum * row_sum
    new_sum_ref[...] = new_sum
    new_table_ref[...] = table_ref[...] - LEARN_RATE * row_sum / (jnp.sqrt(new_sum) + EPSILON)


def whole(shape):
    return pl.BlockSpec(shape, lambda *_: (0,) * len(shape))


def body(hidden, out_grad, memory, w_key, w_value, row_owner, row_slot, mem_table, adagrad_sum):
    tokens, width = hidden.shape
    depth = memory.shape[1]
    quarter = tokens // 4
    me = lax.axis_index("tensor").astype(jnp.int32)
    at = me.reshape(1)
    tile = 256
    tiles = tokens // tile

    def by_rows(cols):
        return pl.BlockSpec((tile, cols), lambda i: (i, 0))

    part_spec = pl.BlockSpec((2, tile), lambda i: (0, i))
    proj_key, part = pl.pallas_call(
        forward_kernel,
        grid=(tiles,),
        in_specs=[
            by_rows(depth),
            by_rows(width),
            by_rows(width),
            whole((depth, width)),
            whole((depth, width)),
        ],
        out_specs=[by_rows(width), part_spec],
        out_shape=[
            jax.ShapeDtypeStruct((tokens, width), F32),
            jax.ShapeDtypeStruct((2, tokens), F32),
        ],
        compiler_params=params(40),
        cost_estimate=cost(4 * tokens * depth * width, 12 << 20),
        name="forward",
    )(memory, hidden, out_grad, w_key, w_value)
    parts = [part] + [
        lax.ppermute(part, "tensor", [(i, (i + step) % 4) for i in range(4)]) for step in (1, 2, 3)
    ]

    ranks, sent = pl.pallas_call(
        ranks_kernel,
        grid_spec=pltpu.PrefetchScalarGridSpec(
            num_scalar_prefetch=1,
            grid=(1,),
            in_specs=[pl.BlockSpec((HEADS, quarter), lambda i, s: (0, s[0]))] * 2,
            out_specs=[whole((HEADS, quarter)), whole((128, 128))],
        ),
        out_shape=[
            jax.ShapeDtypeStruct((HEADS, quarter), jnp.int32),
            jax.ShapeDtypeStruct((128, 128), F32),
        ],
        compiler_params=params(16),
        cost_estimate=cost(200 << 20, 1 << 20),
        name="ranks",
    )(at, row_owner.T, row_slot.T)

    both, hidden_grad = pl.pallas_call(
        gate_kernel,
        grid=(tiles,),
        in_specs=[part_spec] * 4 + [by_rows(width)] * 3,
        out_specs=[by_rows(2 * width), by_rows(width)],
        out_shape=[
            jax.ShapeDtypeStruct((tokens, 2 * width), BF16),
            jax.ShapeDtypeStruct((tokens, width), BF16),
        ],
        compiler_params=params(32),
        cost_estimate=cost(8 * tokens * width, 9 << 20),
        name="gate",
    )(*parts, hidden, out_grad, proj_key)

    def memory_grad(first, steps, name):
        out = pl.BlockSpec((1, quarter, width), lambda p, s: (p, 0, 0))
        return pl.pallas_call(
            memory_grad_kernel,
            grid_spec=pltpu.PrefetchScalarGridSpec(
                num_scalar_prefetch=1,
                grid=(steps,),
                in_specs=[
                    pl.BlockSpec((quarter, 2 * width), lambda p, s: ((s[0] + 7 - first - p) % 4, 0)),
                    pl.BlockSpec((quarter, 2 * width), lambda p, s: ((s[0] + 1 + first + p) % 4, 0)),
                    whole((depth, width)),
                    whole((depth, width)),
                ],
                out_specs=[out, out],
            ),
            out_shape=[jax.ShapeDtypeStruct((steps, quarter, width), F32)] * 2,
            compiler_params=params(40),
            cost_estimate=cost(
                4 * steps * quarter * depth * width, (4 << 20) + steps * (2 << 20)
            ),
            name=name,
        )(at, both, both, w_key, w_value)

    first_left, first_right = memory_grad(0, 1, "memory_grad_first")
    left = [first_left[0, :128], first_left[0, 128:]]
    right = [first_right[0, :128], first_right[0, 128:]]
    rest_left, rest_right = memory_grad(1, 3, "memory_grad_rest")
    up = [(i, (i + 1) % 4) for i in range(4)]
    down = [(i, (i + 3) % 4) for i in range(4)]
    for step in range(3):
        for piece in range(2):
            rows = slice(piece * 128, (piece + 1) * 128)
            left[piece] = lax.ppermute(left[piece], "tensor", up) + rest_left[step, rows]
            right[piece] = lax.ppermute(right[piece], "tensor", down) + rest_right[step, rows]
    left = jnp.concatenate(left, axis=0)
    right = jnp.concatenate(right, axis=0)

    weight_tile = 256
    both_grads = pl.pallas_call(
        weight_grad_kernel,
        grid=(depth // weight_tile,),
        in_specs=[
            pl.BlockSpec((tokens, weight_tile), lambda i: (0, i)),
            whole((tokens, 2 * width)),
        ],
        out_specs=pl.BlockSpec((weight_tile, 2 * width), lambda i: (i, 0)),
        out_shape=jax.ShapeDtypeStruct((depth, 2 * width), F32),
        compiler_params=params(40),
        cost_estimate=cost(4 * tokens * depth * width, 12 << 20),
        name="weight_grad",
    )(memory, both)
    both_grads = lax.psum_scatter(both_grads, "dp", scatter_dimension=0, tiled=True)
    key_weight_grad = both_grads[:, :width]
    value_weight_grad = both_grads[:, width:]

    packed = pl.pallas_call(
        pack_kernel,
        grid=(4,),
        in_specs=[
            whole((quarter, width)),
            whole((quarter, width)),
            whole((HEADS, quarter)),
            whole((HEADS, quarter)),
            whole((128, 128)),
        ],
        out_specs=whole((128 * CHUNK, 128)),
        out_shape=jax.ShapeDtypeStruct((128 * CHUNK, 128), F32),
        scratch_shapes=[
            pltpu.VMEM((GROUP * 128, HEADS * quarter), BF16),
            pltpu.VMEM((HEADS * quarter, 512), BF16),
            pltpu.VMEM((GROUP * 128, 128), F32),
        ],
        compiler_params=params(48),
        cost_estimate=cost(2 * 4096 * 2048 * 512, 6 << 20),
        name="pack",
    )(left, right, ranks_owner(row_owner, me, quarter), ranks, sent)
    received = lax.all_to_all(
        packed.reshape(128, 1, CHUNK * 128),
        ("dp", "tensor"),
        split_axis=0,
        concat_axis=0,
        tiled=True,
    ).reshape(128 * CHUNK, 128)
    owned = mem_table.shape[0]
    table_spec = whole((EH, owned))
    new_table, new_sum = pl.pallas_call(
        update_kernel,
        grid=(1,),
        in_specs=[whole((128 * CHUNK, 128)), table_spec, table_spec],
        out_specs=[table_spec, table_spec],
        out_shape=[jax.ShapeDtypeStruct((EH, owned), F32)] * 2,
        scratch_shapes=[
            pltpu.VMEM((2 * EH, CAP * 128), BF16),
            pltpu.VMEM((CAP * 128, owned), BF16),
        ],
        compiler_params=params(48),
        cost_estimate=cost(4 * EH * 4096 * 512, 5 << 20),
        name="update",
    )(received, mem_table.T, adagrad_sum.T)
    return (hidden_grad, key_weight_grad, value_weight_grad, new_table.T, new_sum.T)


def ranks_owner(row_owner, me, quarter):
    return lax.dynamic_slice_in_dim(row_owner, me * quarter, quarter, 0).T


def solution(mesh):
    return jax.shard_map(
        body,
        mesh=mesh,
        in_specs=(
            P("dp", "tensor"),
            P("dp", "tensor"),
            P("dp", None),
            P(None, "tensor"),
            P(None, "tensor"),
            P("dp", None),
            P("dp", None),
            P(("dp", "tensor"), None),
            P(("dp", "tensor"), None),
        ),
        out_specs=(
            P("dp", "tensor"),
            P("dp", "tensor"),
            P("dp", "tensor"),
            P(("dp", "tensor"), None),
            P(("dp", "tensor"), None),
        ),
        check_vma=False,
    )
```

```python
import functools

import jax
import jax.numpy as jnp
from jax import lax
from jax.experimental import pallas as pl
from jax.experimental.pallas import tpu as pltpu
from jax.sharding import PartitionSpec as P

D = 2560
HEADS = 8
EH = 160
MAIN = 128
TAIL = EH - MAIN
CAP = 32
GROUP = CAP // 4
CHUNK = CAP + GROUP + 1
LEARN_RATE = 0.5
EPSILON = 1e-06
F32 = jnp.float32
BF16 = jnp.bfloat16
OVER_ROWS = (((0,), (0,)), ((), ()))
OVER_LANES = (((1,), (1,)), ((), ()))


def params(mib):
    return pltpu.CompilerParams(vmem_limit_bytes=mib << 20)


def cost(flops, moved):
    return pl.CostEstimate(flops=flops, bytes_accessed=moved, transcendentals=0)


def row_sums(x):
    lanes = x[:, :128]
    for at in range(128, x.shape[1], 128):
        lanes = lanes + x[:, at : at + 128]
    return jnp.sum(lanes.T, axis=0, keepdims=True)


def as_columns(row, width):
    column = jnp.broadcast_to(row, (128, row.shape[1])).T
    return jnp.concatenate([column] * (width // 128), axis=1)


def ranks_kernel(at_ref, owners_ref, slots_ref, select_ref, group_ref, sent_ref):
    count = owners_ref.shape[1]
    owners = owners_ref[...]
    slot_plus = slots_ref[...] + 1
    ids = lax.broadcasted_iota(jnp.int32, (128, count), 0)
    hits = jnp.zeros((128, count), F32)
    for h in range(HEADS):
        hits = hits + jnp.where(owners[h : h + 1] == ids, 1.0, 0.0)
    earlier = lax.broadcasted_iota(jnp.int32, (count, count), 0) < lax.broadcasted_iota(
        jnp.int32, (count, count), 1
    )
    before = jnp.dot(
        hits.astype(BF16), jnp.where(earlier, 1.0, 0.0).astype(BF16), preferred_element_type=F32
    )
    high = jnp.zeros((128, 128), F32)
    low = jnp.zeros((128, 128), F32)
    for h in range(HEADS):
        match = owners[h : h + 1] == ids
        rank = jnp.sum(jnp.where(match, before, 0.0), axis=0, keepdims=True).astype(jnp.int32)
        place = jnp.where(rank == ids, 1.0, 0.0).astype(BF16)
        slot = slot_plus[h : h + 1]
        upper = jnp.where(match, (slot // 16).astype(F32), 0.0).astype(BF16)
        lower = jnp.where(match, (slot % 16).astype(F32), 0.0).astype(BF16)
        high = high + lax.dot_general(upper, place, OVER_LANES, preferred_element_type=F32)
        low = low + lax.dot_general(lower, place, OVER_LANES, preferred_element_type=F32)
        columns = slice(h * count, (h + 1) * count)
        group_ref[columns, :] = jnp.broadcast_to((rank // GROUP).astype(F32), (128, count)).T
        within = jnp.where(match, rank % GROUP, -1)
        for k in range(GROUP):
            select_ref[k * 128 : (k + 1) * 128, columns] = jnp.where(within == k, 1.0, 0.0).astype(
                BF16
            )
    sent_ref[...] = 16.0 * high + low


def forward_kernel(
    at_ref, memory_ref, hidden_ref, grad_ref, wk_ref, wv_ref, key_ref, part_ref, first_ref
):
    @pl.when(pl.program_id(0) == at_ref[0])
    def _():
        width = hidden_ref.shape[1]
        first_ref[:, :width] = hidden_ref[...]
        first_ref[:, width:] = grad_ref[...]

    memory = memory_ref[...]
    proj_key = jnp.dot(memory, wk_ref[...], preferred_element_type=F32)
    key_ref[...] = proj_key
    part_ref[0:1, :] = row_sums(hidden_ref[...].astype(F32) * proj_key)
    proj_value = jnp.dot(memory, wv_ref[...], preferred_element_type=F32)
    part_ref[1:2, :] = row_sums(grad_ref[...].astype(F32) * proj_value)


def gate_columns(total, width):
    root = jnp.sqrt(jnp.full((1, 1), D, F32))
    gate = jax.nn.sigmoid(total[0:1] / root)
    score = total[1:2] * gate * (1.0 - gate) / root
    return as_columns(gate, width), as_columns(score, width)


def backward_tile(total, hidden_ref, grad_ref):
    gates, scores = gate_columns(total, hidden_ref.shape[1])
    key_grad = (scores * hidden_ref[...].astype(F32)).astype(BF16)
    value_grad = (gates * grad_ref[...].astype(F32)).astype(BF16)
    return key_grad, value_grad, scores


def memory_grad_tile(key_grad, value_grad, wk_ref, wv_ref, top_ref, low_ref):
    top = top_ref.shape[0]
    for h in range(HEADS):
        rows = slice(h * EH, (h + 1) * EH)
        head = lax.dot_general(
            key_grad, wk_ref[rows, :], OVER_LANES, preferred_element_type=F32
        ) + lax.dot_general(value_grad, wv_ref[rows, :], OVER_LANES, preferred_element_type=F32)
        main = slice(h * MAIN, (h + 1) * MAIN)
        tail = slice(HEADS * MAIN + h * TAIL, HEADS * MAIN + (h + 1) * TAIL)
        top_ref[:, main] = head[:top, :MAIN]
        top_ref[:, tail] = head[:top, MAIN:]
        low_ref[:, main] = head[top:, :MAIN]
        low_ref[:, tail] = head[top:, MAIN:]


def first_kernel(
    at_ref, p0, p1, p2, p3, first_ref, wk_ref, wv_ref, top_ref, low_ref, total_ref
):
    total_ref[...] = (p0[...] + p1[...]) + (p2[...] + p3[...])
    count, width = first_ref.shape[0], first_ref.shape[1] // 2
    total = total_ref[:, pl.ds(pl.multiple_of(at_ref[0] * count, count), count)]
    key_grad, value_grad, _ = backward_tile(
        total, first_ref.at[:, :width], first_ref.at[:, width:]
    )
    memory_grad_tile(key_grad, value_grad, wk_ref, wv_ref, top_ref, low_ref)


def gate_kernel(total_ref, hidden_ref, grad_ref, both_ref):
    width = hidden_ref.shape[1]
    key_grad, value_grad, _ = backward_tile(total_ref[...], hidden_ref, grad_ref)
    both_ref[:, :width] = key_grad
    both_ref[:, width:] = value_grad


def hidden_grad_kernel(total_ref, key_ref, out_ref):
    _, scores = gate_columns(total_ref[...], key_ref.shape[1])
    out_ref[...] = (scores * key_ref[...]).astype(BF16)


def rest_kernel(at_ref, both_ref, wk_ref, wv_ref, top_ref, low_ref):
    width = wk_ref.shape[1]
    memory_grad_tile(
        both_ref[:, :width], both_ref[:, width:], wk_ref, wv_ref, top_ref.at[0], low_ref.at[0]
    )


def weight_grad_kernel(at_ref, memory_ref, both_ref, mine_ref, other_ref):
    i = pl.program_id(0)
    block = mine_ref.shape[0] // 16
    rows = memory_ref.shape[1]
    me_x, me_z, me_core = at_ref[0], at_ref[1], at_ref[2]

    def order(r):
        return jnp.where(r == 0, 0, jnp.where(r == 3, 1, r + 1))

    found = lax.dot_general(
        memory_ref[...], both_ref[...], OVER_ROWS, preferred_element_type=F32
    )
    for p in range(rows // block):
        x = order((i * 2 + p // 8) ^ me_x)
        z = order((p % 8 // 2) ^ me_z)
        place = x * 4 + z if p % 2 == 0 else z * 4 + x
        to = pl.ds(pl.multiple_of(place * block, 8), block)
        value = found[p * block : (p + 1) * block]

        @pl.when(me_core == p % 2)
        def _():
            mine_ref[to, :] = value

        @pl.when(me_core != p % 2)
        def _():
            other_ref[to, :] = value


def pack_kernel(top_ref, low_ref, select_ref, group_ref, sent_ref, out_ref, rows):
    count = top_ref.shape[0] + low_ref.shape[0]

    def summed(cols):
        return jnp.concatenate([top_ref[:, cols], low_ref[:, cols]], axis=0)

    lane_group = lax.broadcasted_iota(jnp.int32, (count, 128), 1) // TAIL
    for j in range(5):
        for h in range(HEADS):
            group = group_ref[h * count : (h + 1) * count, :]
            if j < 4:
                value = jnp.where(group == j, summed(slice(h * MAIN, (h + 1) * MAIN)), 0.0)
            else:
                at = HEADS * MAIN + h * TAIL
                tail = summed(slice(at, at + TAIL))
                tail = jnp.concatenate([tail] * 4, axis=1)
                value = jnp.where(group == lane_group.astype(F32), tail, 0.0)
            top = value.astype(BF16)
            rows[j, h * count : (h + 1) * count, :MAIN] = top
            rows[j, h * count : (h + 1) * count, MAIN:] = (value - top.astype(F32)).astype(BF16)
        found = jnp.dot(select_ref[...], rows[j], preferred_element_type=F32)
        found = found[:, :MAIN] + found[:, MAIN:]
        for k in range(GROUP):
            out_ref[pl.ds(j * GROUP + k, 128, stride=CHUNK), :] = found[k * 128 : (k + 1) * 128]
    out_ref[pl.ds(CAP + GROUP, 128, stride=CHUNK), :] = sent_ref[...]


def update_kernel(got_ref, table_ref, sums_ref, new_table_ref, new_sum_ref, values, select):
    owned = table_ref.shape[1]
    slots = got_ref[pl.ds(CAP + GROUP, 128, stride=CHUNK), :]
    ids = (lax.broadcasted_iota(jnp.int32, (128, owned), 1) + 1).astype(F32)
    for k in range(CAP):
        at = slice(k * 128, (k + 1) * 128)
        select[at, :] = jnp.where(slots[:, k : k + 1] == ids, 1.0, 0.0).astype(BF16)
        main = got_ref[pl.ds(k, 128, stride=CHUNK), :].T
        top = main.astype(BF16)
        values[:MAIN, at] = top
        values[EH : EH + MAIN, at] = (main - top.astype(F32)).astype(BF16)
    for k in range(GROUP):
        tail = got_ref[pl.ds(CAP + k, 128, stride=CHUNK), :].T
        top = tail.astype(BF16)
        rest = (tail - top.astype(F32)).astype(BF16)
        for j in range(4):
            at = slice((j * GROUP + k) * 128, (j * GROUP + k + 1) * 128)
            values[MAIN:EH, at] = top[j * TAIL : (j + 1) * TAIL]
            values[EH + MAIN :, at] = rest[j * TAIL : (j + 1) * TAIL]
    both = jnp.dot(values[...], select[...], preferred_element_type=F32)
    row_sum = both[:EH] + both[EH:]
    new_sum = sums_ref[...] + row_sum * row_sum
    new_sum_ref[...] = new_sum
    new_table_ref[...] = table_ref[...] - LEARN_RATE * row_sum / (jnp.sqrt(new_sum) + EPSILON)


def whole(shape):
    return pl.BlockSpec(shape, lambda *_: (0,) * len(shape))


def body(hidden, out_grad, memory, w_key, w_value, row_owner, row_slot, mem_table, adagrad_sum):
    tokens, width = hidden.shape
    depth = memory.shape[1]
    quarter = tokens // 4
    tile = 256
    tiles = tokens // tile

    position = lax.axis_index("dp").astype(jnp.int32)
    core = position & 1
    place = jnp.stack([position >> 3, (position >> 1) & 3, core])
    at = jnp.stack([lax.axis_index("tensor").astype(jnp.int32), core])

    def quarter_at(p, s):
        return (s[0] + 4 + (1 + p) * (2 * s[1] - 1)) & 3

    start = quarter_at(0, at).reshape(1)

    def by_rows(cols):
        return pl.BlockSpec((tile, cols), lambda i, s: (i, 0))

    chunk = whole((quarter, 2 * width))
    proj_key, part, first_both = pl.pallas_call(
        forward_kernel,
        grid_spec=pltpu.PrefetchScalarGridSpec(
            num_scalar_prefetch=1,
            grid=(tiles,),
            in_specs=[
                by_rows(depth),
                by_rows(width),
                by_rows(width),
                whole((depth, width)),
                whole((depth, width)),
            ],
            out_specs=[
                by_rows(width),
                pl.BlockSpec((2, tile), lambda i, s: (0, i)),
                chunk,
            ],
        ),
        out_shape=[
            jax.ShapeDtypeStruct((tokens, width), F32),
            jax.ShapeDtypeStruct((2, tokens), F32),
            jax.ShapeDtypeStruct((quarter, 2 * width), BF16),
        ],
        compiler_params=params(58),
        cost_estimate=cost(4 * tokens * depth * width, 12 << 20),
        name="forward",
    )(start, memory, hidden, out_grad, w_key, w_value)
    parts = [part] + [
        lax.ppermute(part, "tensor", [(i, (i + step) % 4) for i in range(4)]) for step in (1, 2, 3)
    ]

    def swapped(value, bits):
        def goal(i):
            dp, tensor = i // 4, i % 4
            by = bits[dp % 2]
            return (dp ^ by[0]) * 4 + (tensor ^ by[1])

        return lax.ppermute(value, ("dp", "tensor"), [(i, goal(i)) for i in range(128)])

    def turned(value):
        def goal(i):
            return i // 4 * 4 + (i + (1, 3)[i // 4 % 2]) % 4

        return lax.ppermute(value, ("dp", "tensor"), [(i, goal(i)) for i in range(128)])

    def tile_spec(cols):
        return pl.BlockSpec((quarter, cols), lambda p, s: (quarter_at(p, s), 0))

    weights = [whole((depth, width))] * 2
    part_whole = whole((2, tokens))
    top = 136
    low = quarter - top
    first_top, first_low, total = pl.pallas_call(
        first_kernel,
        grid_spec=pltpu.PrefetchScalarGridSpec(
            num_scalar_prefetch=1,
            grid=(1,),
            in_specs=[part_whole] * 4 + [chunk] + weights,
            out_specs=[whole((top, depth)), whole((low, depth)), part_whole],
        ),
        out_shape=[
            jax.ShapeDtypeStruct((top, depth), F32),
            jax.ShapeDtypeStruct((low, depth), F32),
            jax.ShapeDtypeStruct((2, tokens), F32),
        ],
        compiler_params=params(20),
        cost_estimate=cost(4 * quarter * depth * width, 6 << 20),
        name="first",
    )(start, *parts, first_both, w_key, w_value)

    def by_rows(cols):
        return pl.BlockSpec((quarter, cols), lambda i: (i, 0))

    total_spec = pl.BlockSpec((2, quarter), lambda i: (0, i))
    both = pl.pallas_call(
        gate_kernel,
        grid=(4,),
        in_specs=[total_spec] + [by_rows(width)] * 2,
        out_specs=by_rows(2 * width),
        out_shape=jax.ShapeDtypeStruct((tokens, 2 * width), BF16),
        compiler_params=params(24),
        cost_estimate=cost(1, 1),
        name="gate",
    )(total, hidden, out_grad)

    grad_spec = whole((depth // 2, 2 * width))
    mine, other = pl.pallas_call(
        weight_grad_kernel,
        grid_spec=pltpu.PrefetchScalarGridSpec(
            num_scalar_prefetch=1,
            grid=(2,),
            in_specs=[
                pl.BlockSpec((tokens, depth // 2), lambda i, s: (0, i)),
                whole((tokens, 2 * width)),
            ],
            out_specs=[grad_spec, grad_spec],
        ),
        out_shape=[jax.ShapeDtypeStruct((depth // 2, 2 * width), F32)] * 2,
        compiler_params=params(32),
        cost_estimate=cost(1, 1),
        name="weight_grad",
    )(place, memory, both)
    late, _ = lax.optimization_barrier((both, other))
    rest_top, rest_low = pl.pallas_call(
        rest_kernel,
        grid_spec=pltpu.PrefetchScalarGridSpec(
            num_scalar_prefetch=1,
            grid=(3,),
            in_specs=[
                pl.BlockSpec((quarter, 2 * width), lambda p, s: (quarter_at(p + 1, s), 0)),
                *weights,
            ],
            out_specs=[
                pl.BlockSpec((1, top, depth), lambda p, s: (p, 0, 0)),
                pl.BlockSpec((1, low, depth), lambda p, s: (p, 0, 0)),
            ],
        ),
        out_shape=[
            jax.ShapeDtypeStruct((3, top, depth), F32),
            jax.ShapeDtypeStruct((3, low, depth), F32),
        ],
        compiler_params=params(24),
        cost_estimate=cost(1, 1),
        name="rest",
    )(at, late, w_key, w_value)

    def folded(value, bits):
        half = value.shape[0] // 2
        return value[:half] + swapped(value[half:], bits)

    moved_top = turned(first_top) + rest_top[0]
    moved_low = turned(first_low) + rest_low[0]
    moved_top, owners, slots = lax.optimization_barrier((moved_top, row_owner.T, row_slot.T))
    passed_top = turned(moved_top)
    passed_low = turned(moved_low)
    select, group, sent = pl.pallas_call(
        ranks_kernel,
        grid_spec=pltpu.PrefetchScalarGridSpec(
            num_scalar_prefetch=1,
            grid=(1,),
            in_specs=[pl.BlockSpec((HEADS, quarter), lambda i, s: (0, s[0]))] * 2,
            out_specs=[
                whole((GROUP * 128, HEADS * quarter)),
                whole((HEADS * quarter, 128)),
                whole((128, 128)),
            ],
        ),
        out_shape=[
            jax.ShapeDtypeStruct((GROUP * 128, HEADS * quarter), BF16),
            jax.ShapeDtypeStruct((HEADS * quarter, 128), F32),
            jax.ShapeDtypeStruct((128, 128), F32),
        ],
        compiler_params=params(32),
        cost_estimate=cost(1 << 36, 1 << 27),
        name="ranks",
    )(at, owners, slots)
    mine, select = lax.optimization_barrier((mine, select))
    pair = mine + swapped(other, ((1, 0), (1, 0)))
    rest_low, pair = lax.optimization_barrier((rest_low, pair))
    moved_top = turned(passed_top + rest_top[1])
    moved_low = turned(passed_low + rest_low[1])
    grads = folded(pair, ((8, 0), (2, 0)))
    rest_low, grads = lax.optimization_barrier((rest_low, grads))
    sum_top = moved_top + rest_top[2]
    sum_low = moved_low + rest_low[2]
    grads = folded(grads, ((24, 0), (6, 0)))
    sum_low, grads = lax.optimization_barrier((sum_low, grads))
    grads = folded(grads, ((2, 0), (8, 0)))

    packed = pl.pallas_call(
        pack_kernel,
        grid=(1,),
        in_specs=[
            whole((top, depth)),
            whole((low, depth)),
            whole((GROUP * 128, HEADS * quarter)),
            whole((HEADS * quarter, 128)),
            whole((128, 128)),
        ],
        out_specs=whole((128 * CHUNK, 128)),
        out_shape=jax.ShapeDtypeStruct((128 * CHUNK, 128), F32),
        scratch_shapes=[pltpu.VMEM((5, HEADS * quarter, 256), BF16)],
        compiler_params=params(32),
        cost_estimate=cost(2 * 1024 * 2048 * 1280, 12 << 20),
        name="pack",
    )(sum_top, sum_low, select, group, sent)
    packed, grads, total = lax.optimization_barrier((packed, grads, total))
    hidden_grad = pl.pallas_call(
        hidden_grad_kernel,
        grid=(4,),
        in_specs=[total_spec, by_rows(width)],
        out_specs=by_rows(width),
        out_shape=jax.ShapeDtypeStruct((tokens, width), BF16),
        compiler_params=params(24),
        cost_estimate=cost(2 * tokens * width, 4 << 20),
        name="hidden_grad",
    )(total, proj_key)
    received = lax.all_to_all(
        packed.reshape(128, 1, CHUNK * 128),
        ("dp", "tensor"),
        split_axis=0,
        concat_axis=0,
        tiled=True,
    ).reshape(128 * CHUNK, 128)
    received, hidden_grad = lax.optimization_barrier((received, hidden_grad))
    owned = mem_table.shape[0]
    table_spec = whole((EH, owned))
    new_table, new_sum = pl.pallas_call(
        update_kernel,
        grid=(1,),
        in_specs=[whole((128 * CHUNK, 128)), table_spec, table_spec],
        out_specs=[table_spec, table_spec],
        out_shape=[jax.ShapeDtypeStruct((EH, owned), F32)] * 2,
        scratch_shapes=[
            pltpu.VMEM((2 * EH, CAP * 128), BF16),
            pltpu.VMEM((CAP * 128, owned), BF16),
        ],
        compiler_params=params(48),
        cost_estimate=cost(4 * EH * 4096 * 512, 5 << 20),
        name="update",
    )(received, mem_table.T, adagrad_sum.T)
    half = grads.shape[0] // 2
    last = swapped(grads[half:], ((6, 0), (24, 0)))
    kept, new_table = lax.optimization_barrier((grads[:half], new_table))
    key_weight_grad = kept[:, :width] + last[:, :width]
    value_weight_grad = kept[:, width:] + last[:, width:]
    return (hidden_grad, key_weight_grad, value_weight_grad, new_table.T, new_sum.T)


def solution(mesh):
    return jax.shard_map(
        body,
        mesh=mesh,
        in_specs=(
            P("dp", "tensor"),
            P("dp", "tensor"),
            P("dp", None),
            P(None, "tensor"),
            P(None, "tensor"),
            P("dp", None),
            P("dp", None),
            P(("dp", "tensor"), None),
            P(("dp", "tensor"), None),
        ),
        out_specs=(
            P("dp", "tensor"),
            P("dp", "tensor"),
            P("dp", "tensor"),
            P(("dp", "tensor"), None),
            P(("dp", "tensor"), None),
        ),
        check_vma=False,
    )
```

```python
import functools

import jax
import jax.numpy as jnp
from jax import lax
from jax.experimental import pallas as pl
from jax.experimental.pallas import tpu as pltpu
from jax.sharding import PartitionSpec as P

D = 2560
HEADS = 8
EH = 160
MAIN = 128
TAIL = EH - MAIN
CAP = 32
GROUP = CAP // 4
CHUNK = CAP + GROUP + 1
LEARN_RATE = 0.5
EPSILON = 1e-06
F32 = jnp.float32
BF16 = jnp.bfloat16
OVER_ROWS = (((0,), (0,)), ((), ()))
OVER_LANES = (((1,), (1,)), ((), ()))


def params(mib):
    return pltpu.CompilerParams(vmem_limit_bytes=mib << 20)


def cost(flops, moved):
    return pl.CostEstimate(flops=flops, bytes_accessed=moved, transcendentals=0)


def row_sums(x):
    lanes = x[:, :128]
    for at in range(128, x.shape[1], 128):
        lanes = lanes + x[:, at : at + 128]
    return jnp.sum(lanes.T, axis=0, keepdims=True)


def as_columns(row, width):
    column = jnp.broadcast_to(row, (128, row.shape[1])).T
    return jnp.concatenate([column] * (width // 128), axis=1)


def ranks_kernel(at_ref, owners_ref, slots_ref, select_ref, group_ref, sent_ref):
    count = owners_ref.shape[1]
    owners = owners_ref[...]
    slot_plus = slots_ref[...] + 1
    ids = lax.broadcasted_iota(jnp.int32, (128, count), 0)
    hits = jnp.zeros((128, count), F32)
    for h in range(HEADS):
        hits = hits + jnp.where(owners[h : h + 1] == ids, 1.0, 0.0)
    earlier = lax.broadcasted_iota(jnp.int32, (count, count), 0) < lax.broadcasted_iota(
        jnp.int32, (count, count), 1
    )
    before = jnp.dot(
        hits.astype(BF16), jnp.where(earlier, 1.0, 0.0).astype(BF16), preferred_element_type=F32
    )
    high = jnp.zeros((128, 128), F32)
    low = jnp.zeros((128, 128), F32)
    for h in range(HEADS):
        match = owners[h : h + 1] == ids
        rank = jnp.sum(jnp.where(match, before, 0.0), axis=0, keepdims=True).astype(jnp.int32)
        place = jnp.where(rank == ids, 1.0, 0.0).astype(BF16)
        slot = slot_plus[h : h + 1]
        upper = jnp.where(match, (slot // 16).astype(F32), 0.0).astype(BF16)
        lower = jnp.where(match, (slot % 16).astype(F32), 0.0).astype(BF16)
        high = high + lax.dot_general(upper, place, OVER_LANES, preferred_element_type=F32)
        low = low + lax.dot_general(lower, place, OVER_LANES, preferred_element_type=F32)
        columns = slice(h * count, (h + 1) * count)
        group_ref[columns, :] = jnp.broadcast_to((rank // GROUP).astype(F32), (128, count)).T
        within = jnp.where(match, rank % GROUP, -1)
        for k in range(GROUP):
            select_ref[k * 128 : (k + 1) * 128, columns] = jnp.where(within == k, 1.0, 0.0).astype(
                BF16
            )
    sent_ref[...] = 16.0 * high + low


def forward_kernel(
    at_ref, memory_ref, hidden_ref, grad_ref, wk_ref, wv_ref, part_ref, first_ref
):
    @pl.when(pl.program_id(0) == at_ref[0])
    def _():
        width = hidden_ref.shape[1]
        first_ref[:, :width] = hidden_ref[...]
        first_ref[:, width:] = grad_ref[...]

    memory = memory_ref[...]
    proj_key = jnp.dot(memory, wk_ref[...], preferred_element_type=F32)
    part_ref[0:1, :] = row_sums(hidden_ref[...].astype(F32) * proj_key)
    proj_value = jnp.dot(memory, wv_ref[...], preferred_element_type=F32)
    part_ref[1:2, :] = row_sums(grad_ref[...].astype(F32) * proj_value)


def gate_columns(total, width):
    root = jnp.sqrt(jnp.full((1, 1), D, F32))
    gate = jax.nn.sigmoid(total[0:1] / root)
    score = total[1:2] * gate * (1.0 - gate) / root
    return as_columns(gate, width), as_columns(score, width)


def summed_parts(part_refs, at=slice(None)):
    p0, p1, p2, p3 = (ref[:, at] for ref in part_refs)
    return (p0 + p1) + (p2 + p3)


def memory_grad_tile(key_grad, value_grad, wk_ref, wv_ref, *out_refs):
    for h in range(HEADS):
        rows = slice(h * EH, (h + 1) * EH)
        head = lax.dot_general(
            key_grad, wk_ref[rows, :], OVER_LANES, preferred_element_type=F32
        ) + lax.dot_general(value_grad, wv_ref[rows, :], OVER_LANES, preferred_element_type=F32)
        tail = slice(HEADS * MAIN + h * TAIL, HEADS * MAIN + (h + 1) * TAIL)
        at = 0
        for out_ref in out_refs:
            here = slice(at, at + out_ref.shape[0])
            out_ref[:, h * MAIN : (h + 1) * MAIN] = head[here, :MAIN]
            out_ref[:, tail] = head[here, MAIN:]
            at += out_ref.shape[0]


def first_kernel(at_ref, p0, p1, p2, p3, first_ref, wk_ref, wv_ref, top_ref, low_ref):
    count, width = first_ref.shape[0], first_ref.shape[1] // 2
    tile = pl.ds(pl.multiple_of(at_ref[0] * count, count), count)
    gates, scores = gate_columns(summed_parts((p0, p1, p2, p3), tile), width)
    key_grad = (scores * first_ref[:, :width].astype(F32)).astype(BF16)
    value_grad = (gates * first_ref[:, width:].astype(F32)).astype(BF16)
    memory_grad_tile(key_grad, value_grad, wk_ref, wv_ref, top_ref, low_ref)


def gate_kernel(p0, p1, p2, p3, hidden_ref, grad_ref, both_ref):
    width = hidden_ref.shape[1]
    gates, scores = gate_columns(summed_parts((p0, p1, p2, p3)), width)
    both_ref[:, :width] = (scores * hidden_ref[...].astype(F32)).astype(BF16)
    both_ref[:, width:] = (gates * grad_ref[...].astype(F32)).astype(BF16)


def hidden_grad_kernel(p0, p1, p2, p3, memory_ref, wk_ref, out_ref):
    _, scores = gate_columns(summed_parts((p0, p1, p2, p3)), out_ref.shape[1])
    proj_key = jnp.dot(memory_ref[...], wk_ref[...], preferred_element_type=F32)
    out_ref[...] = (scores * proj_key).astype(BF16)


def rest_kernel(at_ref, both_ref, wk_ref, wv_ref, top_ref, low_ref):
    width = wk_ref.shape[1]
    memory_grad_tile(
        both_ref[:, :width], both_ref[:, width:], wk_ref, wv_ref, top_ref.at[0], low_ref.at[0]
    )


def weight_grad_kernel(at_ref, memory_ref, both_ref, mine_ref, other_ref):
    i = pl.program_id(0)
    block = mine_ref.shape[0] // 16
    rows = memory_ref.shape[1]
    me_x, me_z, me_core = at_ref[0], at_ref[1], at_ref[2]

    def order(r):
        return jnp.where(r == 0, 0, jnp.where(r == 3, 1, r + 1))

    found = lax.dot_general(
        memory_ref[...], both_ref[...], OVER_ROWS, preferred_element_type=F32
    )
    for p in range(rows // block):
        x = order((i * 2 + p // 8) ^ me_x)
        z = order((p % 8 // 2) ^ me_z)
        place = x * 4 + z if p % 2 == 0 else z * 4 + x
        to = pl.ds(pl.multiple_of(place * block, 8), block)
        value = found[p * block : (p + 1) * block]

        @pl.when(me_core == p % 2)
        def _():
            mine_ref[to, :] = value

        @pl.when(me_core != p % 2)
        def _():
            other_ref[to, :] = value


def pack_kernel(top_ref, low_ref, select_ref, group_ref, sent_ref, out_ref, rows):
    count = top_ref.shape[0] + low_ref.shape[0]

    def summed(cols):
        return jnp.concatenate([top_ref[:, cols], low_ref[:, cols]], axis=0)

    lane_group = lax.broadcasted_iota(jnp.int32, (count, 128), 1) // TAIL
    for j in range(5):
        for h in range(HEADS):
            group = group_ref[h * count : (h + 1) * count, :]
            if j < 4:
                value = jnp.where(group == j, summed(slice(h * MAIN, (h + 1) * MAIN)), 0.0)
            else:
                at = HEADS * MAIN + h * TAIL
                tail = summed(slice(at, at + TAIL))
                tail = jnp.concatenate([tail] * 4, axis=1)
                value = jnp.where(group == lane_group.astype(F32), tail, 0.0)
            top = value.astype(BF16)
            rows[j, h * count : (h + 1) * count, :MAIN] = top
            rows[j, h * count : (h + 1) * count, MAIN:] = (value - top.astype(F32)).astype(BF16)
        found = jnp.dot(select_ref[...], rows[j], preferred_element_type=F32)
        found = found[:, :MAIN] + found[:, MAIN:]
        for k in range(GROUP):
            out_ref[pl.ds(j * GROUP + k, 128, stride=CHUNK), :] = found[k * 128 : (k + 1) * 128]
    out_ref[pl.ds(CAP + GROUP, 128, stride=CHUNK), :] = sent_ref[...]


def update_kernel(got_ref, table_ref, sums_ref, new_table_ref, new_sum_ref, values, select):
    owned = table_ref.shape[1]
    slots = got_ref[pl.ds(CAP + GROUP, 128, stride=CHUNK), :]
    ids = (lax.broadcasted_iota(jnp.int32, (128, owned), 1) + 1).astype(F32)
    for k in range(CAP):
        at = slice(k * 128, (k + 1) * 128)
        select[at, :] = jnp.where(slots[:, k : k + 1] == ids, 1.0, 0.0).astype(BF16)
        main = got_ref[pl.ds(k, 128, stride=CHUNK), :].T
        top = main.astype(BF16)
        values[:MAIN, at] = top
        values[EH : EH + MAIN, at] = (main - top.astype(F32)).astype(BF16)
    for k in range(GROUP):
        tail = got_ref[pl.ds(CAP + k, 128, stride=CHUNK), :].T
        top = tail.astype(BF16)
        rest = (tail - top.astype(F32)).astype(BF16)
        for j in range(4):
            at = slice((j * GROUP + k) * 128, (j * GROUP + k + 1) * 128)
            values[MAIN:EH, at] = top[j * TAIL : (j + 1) * TAIL]
            values[EH + MAIN :, at] = rest[j * TAIL : (j + 1) * TAIL]
    both = jnp.dot(values[...], select[...], preferred_element_type=F32)
    row_sum = both[:EH] + both[EH:]
    new_sum = sums_ref[...] + row_sum * row_sum
    new_sum_ref[...] = new_sum
    new_table_ref[...] = table_ref[...] - LEARN_RATE * row_sum / (jnp.sqrt(new_sum) + EPSILON)


def whole(shape):
    return pl.BlockSpec(shape, lambda *_: (0,) * len(shape))


def body(hidden, out_grad, memory, w_key, w_value, row_owner, row_slot, mem_table, adagrad_sum):
    tokens, width = hidden.shape
    depth = memory.shape[1]
    quarter = tokens // 4
    tile = 256
    tiles = tokens // tile

    position = lax.axis_index("dp").astype(jnp.int32)
    core = position & 1
    place = jnp.stack([position >> 3, (position >> 1) & 3, core])
    at = jnp.stack([lax.axis_index("tensor").astype(jnp.int32), core])

    def quarter_at(p, s):
        return (s[0] + 4 + (1 + p) * (2 * s[1] - 1)) & 3

    start = quarter_at(0, at).reshape(1)

    def by_rows(cols):
        return pl.BlockSpec((tile, cols), lambda i, s: (i, 0))

    chunk = whole((quarter, 2 * width))
    part, first_both = pl.pallas_call(
        forward_kernel,
        grid_spec=pltpu.PrefetchScalarGridSpec(
            num_scalar_prefetch=1,
            grid=(tiles,),
            in_specs=[
                by_rows(depth),
                by_rows(width),
                by_rows(width),
                whole((depth, width)),
                whole((depth, width)),
            ],
            out_specs=[
                pl.BlockSpec((2, tile), lambda i, s: (0, i)),
                chunk,
            ],
        ),
        out_shape=[
            jax.ShapeDtypeStruct((2, tokens), F32),
            jax.ShapeDtypeStruct((quarter, 2 * width), BF16),
        ],
        compiler_params=params(53),
        cost_estimate=cost(4 * tokens * depth * width, 12 << 20),
        name="forward",
    )(start, memory, hidden, out_grad, w_key, w_value)
    parts = [part] + [
        lax.ppermute(part, "tensor", [(i, (i + step) % 4) for i in range(4)]) for step in (1, 2, 3)
    ]

    def swapped(value, bits):
        def goal(i):
            dp, tensor = i // 4, i % 4
            by = bits[dp % 2]
            return (dp ^ by[0]) * 4 + (tensor ^ by[1])

        return lax.ppermute(value, ("dp", "tensor"), [(i, goal(i)) for i in range(128)])

    def turned(value):
        def goal(i):
            return i // 4 * 4 + (i + (1, 3)[i // 4 % 2]) % 4

        return lax.ppermute(value, ("dp", "tensor"), [(i, goal(i)) for i in range(128)])

    def tile_spec(cols):
        return pl.BlockSpec((quarter, cols), lambda p, s: (quarter_at(p, s), 0))

    weights = [whole((depth, width))] * 2
    part_whole = whole((2, tokens))
    top = 144
    low = quarter - top

    first_top, first_low = pl.pallas_call(
        first_kernel,
        grid_spec=pltpu.PrefetchScalarGridSpec(
            num_scalar_prefetch=1,
            grid=(1,),
            in_specs=[part_whole] * 4 + [chunk] + weights,
            out_specs=[whole((top, depth)), whole((low, depth))],
        ),
        out_shape=[
            jax.ShapeDtypeStruct((top, depth), F32),
            jax.ShapeDtypeStruct((low, depth), F32),
        ],
        compiler_params=params(20),
        cost_estimate=cost(4 * quarter * depth * width, 6 << 20),
        name="first",
    )(start, *parts, first_both, w_key, w_value)
    parts, _ = lax.optimization_barrier((parts, first_low))

    def by_rows(cols):
        return pl.BlockSpec((quarter, cols), lambda i: (i, 0))

    total_spec = pl.BlockSpec((2, quarter), lambda i: (0, i))
    both = pl.pallas_call(
        gate_kernel,
        grid=(4,),
        in_specs=[total_spec] * 4 + [by_rows(width)] * 2,
        out_specs=by_rows(2 * width),
        out_shape=jax.ShapeDtypeStruct((tokens, 2 * width), BF16),
        compiler_params=params(24),
        cost_estimate=cost(1, 1),
        name="gate",
    )(*parts, hidden, out_grad)

    grad_spec = whole((depth // 2, 2 * width))
    mine, other = pl.pallas_call(
        weight_grad_kernel,
        grid_spec=pltpu.PrefetchScalarGridSpec(
            num_scalar_prefetch=1,
            grid=(2,),
            in_specs=[
                pl.BlockSpec((tokens, depth // 2), lambda i, s: (0, i)),
                whole((tokens, 2 * width)),
            ],
            out_specs=[grad_spec, grad_spec],
        ),
        out_shape=[jax.ShapeDtypeStruct((depth // 2, 2 * width), F32)] * 2,
        compiler_params=params(32),
        cost_estimate=cost(1, 1),
        name="weight_grad",
    )(place, memory, both)
    late, _ = lax.optimization_barrier((both, other))
    rest_top, rest_low = pl.pallas_call(
        rest_kernel,
        grid_spec=pltpu.PrefetchScalarGridSpec(
            num_scalar_prefetch=1,
            grid=(3,),
            in_specs=[
                pl.BlockSpec((quarter, 2 * width), lambda p, s: (quarter_at(p + 1, s), 0)),
                *weights,
            ],
            out_specs=[
                pl.BlockSpec((1, top, depth), lambda p, s: (p, 0, 0)),
                pl.BlockSpec((1, low, depth), lambda p, s: (p, 0, 0)),
            ],
        ),
        out_shape=[
            jax.ShapeDtypeStruct((3, top, depth), F32),
            jax.ShapeDtypeStruct((3, low, depth), F32),
        ],
        compiler_params=params(24),
        cost_estimate=cost(1, 1),
        name="rest",
    )(at, late, w_key, w_value)

    def folded(value, bits):
        half = value.shape[0] // 2
        return value[:half] + swapped(value[half:], bits)

    moved_top = turned(first_top) + rest_top[0]
    moved_low = turned(first_low) + rest_low[0]
    moved_top, moved_low, owners, slots = lax.optimization_barrier(
        (moved_top, moved_low, row_owner.T, row_slot.T)
    )
    passed_top = turned(moved_top)
    passed_low = turned(moved_low)
    select, group, sent = pl.pallas_call(
        ranks_kernel,
        grid_spec=pltpu.PrefetchScalarGridSpec(
            num_scalar_prefetch=1,
            grid=(1,),
            in_specs=[pl.BlockSpec((HEADS, quarter), lambda i, s: (0, s[0]))] * 2,
            out_specs=[
                whole((GROUP * 128, HEADS * quarter)),
                whole((HEADS * quarter, 128)),
                whole((128, 128)),
            ],
        ),
        out_shape=[
            jax.ShapeDtypeStruct((GROUP * 128, HEADS * quarter), BF16),
            jax.ShapeDtypeStruct((HEADS * quarter, 128), F32),
            jax.ShapeDtypeStruct((128, 128), F32),
        ],
        compiler_params=params(32),
        cost_estimate=cost(1 << 36, 1 << 27),
        name="ranks",
    )(at, owners, slots)
    mine, select = lax.optimization_barrier((mine, select))
    pair = mine + swapped(other, ((1, 0), (1, 0)))
    rest_top, rest_low, pair = lax.optimization_barrier((rest_top, rest_low, pair))
    moved_top, moved_low = lax.optimization_barrier(
        (passed_top + rest_top[1], passed_low + rest_low[1])
    )
    moved_top = turned(moved_top)
    moved_low = turned(moved_low)
    grads = folded(pair, ((8, 0), (2, 0)))
    rest_low, grads = lax.optimization_barrier((rest_low, grads))
    sum_top = moved_top + rest_top[2]
    sum_low = moved_low + rest_low[2]
    grads = folded(grads, ((24, 0), (6, 0)))

    packed = pl.pallas_call(
        pack_kernel,
        grid=(1,),
        in_specs=[
            whole((top, depth)),
            whole((low, depth)),
            whole((GROUP * 128, HEADS * quarter)),
            whole((HEADS * quarter, 128)),
            whole((128, 128)),
        ],
        out_specs=whole((128 * CHUNK, 128)),
        out_shape=jax.ShapeDtypeStruct((128 * CHUNK, 128), F32),
        scratch_shapes=[pltpu.VMEM((5, HEADS * quarter, 256), BF16)],
        compiler_params=params(32),
        cost_estimate=cost(2 * 1024 * 2048 * 1280, 12 << 20),
        name="pack",
    )(sum_top, sum_low, select, group, sent)
    packed, grads, parts = lax.optimization_barrier((packed, grads, parts))
    hidden_grad = pl.pallas_call(
        hidden_grad_kernel,
        grid=(4,),
        in_specs=[total_spec] * 4 + [by_rows(depth), whole((depth, width))],
        out_specs=by_rows(width),
        out_shape=jax.ShapeDtypeStruct((tokens, width), BF16),
        compiler_params=params(24),
        cost_estimate=cost(2 * tokens * depth * width, 6 << 20),
        name="hidden_grad",
    )(*parts, memory, w_key)
    received = lax.all_to_all(
        packed.reshape(128, 1, CHUNK * 128),
        ("dp", "tensor"),
        split_axis=0,
        concat_axis=0,
        tiled=True,
    ).reshape(128 * CHUNK, 128)
    grads = folded(grads, ((2, 0), (8, 0)))
    received, hidden_grad, grads = lax.optimization_barrier((received, hidden_grad, grads))
    owned = mem_table.shape[0]
    table_spec = whole((EH, owned))
    new_table, new_sum = pl.pallas_call(
        update_kernel,
        grid=(1,),
        in_specs=[whole((128 * CHUNK, 128)), table_spec, table_spec],
        out_specs=[table_spec, table_spec],
        out_shape=[jax.ShapeDtypeStruct((EH, owned), F32)] * 2,
        scratch_shapes=[
            pltpu.VMEM((2 * EH, CAP * 128), BF16),
            pltpu.VMEM((CAP * 128, owned), BF16),
        ],
        compiler_params=params(48),
        cost_estimate=cost(4 * EH * 4096 * 512, 5 << 20),
        name="update",
    )(received, mem_table.T, adagrad_sum.T)
    half = grads.shape[0] // 2
    last = swapped(grads[half:], ((6, 0), (24, 0)))
    kept, new_table = lax.optimization_barrier((grads[:half], new_table))
    key_weight_grad = kept[:, :width] + last[:, :width]
    value_weight_grad = kept[:, width:] + last[:, width:]
    return (hidden_grad, key_weight_grad, value_weight_grad, new_table.T, new_sum.T)


def solution(mesh):
    return jax.shard_map(
        body,
        mesh=mesh,
        in_specs=(
            P("dp", "tensor"),
            P("dp", "tensor"),
            P("dp", None),
            P(None, "tensor"),
            P(None, "tensor"),
            P("dp", None),
            P("dp", None),
            P(("dp", "tensor"), None),
            P(("dp", "tensor"), None),
        ),
        out_specs=(
            P("dp", "tensor"),
            P("dp", "tensor"),
            P("dp", "tensor"),
            P(("dp", "tensor"), None),
            P(("dp", "tensor"), None),
        ),
        check_vma=False,
    )
```

```python
import functools

import jax
import jax.numpy as jnp
from jax import lax
from jax.experimental import pallas as pl
from jax.experimental.pallas import tpu as pltpu
from jax.sharding import PartitionSpec as P

D = 2560
HEADS = 8
EH = 160
MAIN = 128
TAIL = EH - MAIN
CAP = 32
GROUP = CAP // 4
CHUNK = CAP + GROUP + 1
LEARN_RATE = 0.5
EPSILON = 1e-06
F32 = jnp.float32
BF16 = jnp.bfloat16
OVER_ROWS = (((0,), (0,)), ((), ()))
OVER_LANES = (((1,), (1,)), ((), ()))


def params(mib):
    return pltpu.CompilerParams(vmem_limit_bytes=mib << 20)


def cost(flops, moved):
    return pl.CostEstimate(flops=flops, bytes_accessed=moved, transcendentals=0)


def row_sums(x):
    lanes = x[:, :128]
    for at in range(128, x.shape[1], 128):
        lanes = lanes + x[:, at : at + 128]
    return jnp.sum(lanes.T, axis=0, keepdims=True)


def as_columns(row, width):
    column = jnp.broadcast_to(row, (128, row.shape[1])).T
    return jnp.concatenate([column] * (width // 128), axis=1)


def ranks_kernel(at_ref, owners_ref, slots_ref, select_ref, group_ref, sent_ref):
    count = owners_ref.shape[1]
    owners = owners_ref[...]
    slot_plus = slots_ref[...] + 1
    ids = lax.broadcasted_iota(jnp.int32, (128, count), 0)
    hits = jnp.zeros((128, count), F32)
    for h in range(HEADS):
        hits = hits + jnp.where(owners[h : h + 1] == ids, 1.0, 0.0)
    earlier = lax.broadcasted_iota(jnp.int32, (count, count), 0) < lax.broadcasted_iota(
        jnp.int32, (count, count), 1
    )
    before = jnp.dot(
        hits.astype(BF16), jnp.where(earlier, 1.0, 0.0).astype(BF16), preferred_element_type=F32
    )
    high = jnp.zeros((128, 128), F32)
    low = jnp.zeros((128, 128), F32)
    for h in range(HEADS):
        match = owners[h : h + 1] == ids
        rank = jnp.sum(jnp.where(match, before, 0.0), axis=0, keepdims=True).astype(jnp.int32)
        place = jnp.where(rank == ids, 1.0, 0.0).astype(BF16)
        slot = slot_plus[h : h + 1]
        upper = jnp.where(match, (slot // 16).astype(F32), 0.0).astype(BF16)
        lower = jnp.where(match, (slot % 16).astype(F32), 0.0).astype(BF16)
        high = high + lax.dot_general(upper, place, OVER_LANES, preferred_element_type=F32)
        low = low + lax.dot_general(lower, place, OVER_LANES, preferred_element_type=F32)
        columns = slice(h * count, (h + 1) * count)
        group_ref[columns, :] = jnp.broadcast_to((rank // GROUP).astype(F32), (128, count)).T
        within = jnp.where(match, rank % GROUP, -1)
        for k in range(GROUP):
            select_ref[k * 128 : (k + 1) * 128, columns] = jnp.where(within == k, 1.0, 0.0).astype(
                BF16
            )
    sent_ref[...] = 16.0 * high + low


def forward_kernel(
    at_ref, memory_ref, hidden_ref, grad_ref, wk_ref, wv_ref, part_ref, first_ref
):
    @pl.when(pl.program_id(0) == at_ref[0])
    def _():
        width = hidden_ref.shape[1]
        first_ref[:, :width] = hidden_ref[...]
        first_ref[:, width:] = grad_ref[...]

    memory = memory_ref[...]
    proj_key = jnp.dot(memory, wk_ref[...], preferred_element_type=F32)
    part_ref[0:1, :] = row_sums(hidden_ref[...].astype(F32) * proj_key)
    proj_value = jnp.dot(memory, wv_ref[...], preferred_element_type=F32)
    part_ref[1:2, :] = row_sums(grad_ref[...].astype(F32) * proj_value)


def gate_columns(total, width):
    root = jnp.sqrt(jnp.full((1, 1), D, F32))
    gate = jax.nn.sigmoid(total[0:1] / root)
    score = total[1:2] * gate * (1.0 - gate) / root
    return as_columns(gate, width), as_columns(score, width)


def summed_parts(part_refs, at=slice(None)):
    p0, p1, p2, p3 = (ref[:, at] for ref in part_refs)
    return (p0 + p1) + (p2 + p3)


def memory_grad_tile(key_grad, value_grad, wk_ref, wv_ref, *out_refs):
    for h in range(HEADS):
        rows = slice(h * EH, (h + 1) * EH)
        head = lax.dot_general(
            key_grad, wk_ref[rows, :], OVER_LANES, preferred_element_type=F32
        ) + lax.dot_general(value_grad, wv_ref[rows, :], OVER_LANES, preferred_element_type=F32)
        tail = slice(HEADS * MAIN + h * TAIL, HEADS * MAIN + (h + 1) * TAIL)
        at = 0
        for out_ref in out_refs:
            here = slice(at, at + out_ref.shape[0])
            out_ref[:, h * MAIN : (h + 1) * MAIN] = head[here, :MAIN]
            out_ref[:, tail] = head[here, MAIN:]
            at += out_ref.shape[0]


def first_kernel(at_ref, p0, p1, p2, p3, first_ref, wk_ref, wv_ref, top_ref, low_ref):
    count, width = first_ref.shape[0], first_ref.shape[1] // 2
    tile = pl.ds(pl.multiple_of(at_ref[0] * count, count), count)
    gates, scores = gate_columns(summed_parts((p0, p1, p2, p3), tile), width)
    key_grad = (scores * first_ref[:, :width].astype(F32)).astype(BF16)
    value_grad = (gates * first_ref[:, width:].astype(F32)).astype(BF16)
    memory_grad_tile(key_grad, value_grad, wk_ref, wv_ref, top_ref, low_ref)


def gate_kernel(p0, p1, p2, p3, hidden_ref, grad_ref, both_ref):
    width = hidden_ref.shape[1]
    gates, scores = gate_columns(summed_parts((p0, p1, p2, p3)), width)
    both_ref[:, :width] = (scores * hidden_ref[...].astype(F32)).astype(BF16)
    both_ref[:, width:] = (gates * grad_ref[...].astype(F32)).astype(BF16)


def hidden_grad_kernel(p0, p1, p2, p3, memory_ref, wk_ref, out_ref):
    _, scores = gate_columns(summed_parts((p0, p1, p2, p3)), out_ref.shape[1])
    proj_key = jnp.dot(memory_ref[...], wk_ref[...], preferred_element_type=F32)
    out_ref[...] = (scores * proj_key).astype(BF16)


def rest_kernel(at_ref, both_ref, wk_ref, wv_ref, top_ref, low_ref):
    width = wk_ref.shape[1]
    memory_grad_tile(
        both_ref[:, :width], both_ref[:, width:], wk_ref, wv_ref, top_ref.at[0], low_ref.at[0]
    )


def weight_grad_kernel(at_ref, memory_ref, both_ref, mine_ref, other_ref):
    i = pl.program_id(0)
    block = mine_ref.shape[0] // 16
    rows = memory_ref.shape[1]
    me_x, me_z, me_core = at_ref[0], at_ref[1], at_ref[2]

    def order(r):
        return jnp.where(r == 0, 0, jnp.where(r == 3, 1, r + 1))

    found = lax.dot_general(
        memory_ref[...], both_ref[...], OVER_ROWS, preferred_element_type=F32
    )
    for p in range(rows // block):
        x = order((i * 2 + p // 8) ^ me_x)
        z = order((p % 8 // 2) ^ me_z)
        place = x * 4 + z if p % 2 == 0 else z * 4 + x
        to = pl.ds(pl.multiple_of(place * block, 8), block)
        value = found[p * block : (p + 1) * block]

        @pl.when(me_core == p % 2)
        def _():
            mine_ref[to, :] = value

        @pl.when(me_core != p % 2)
        def _():
            other_ref[to, :] = value


def pack_kernel(top_ref, low_ref, select_ref, group_ref, sent_ref, out_ref, rows):
    count = top_ref.shape[0] + low_ref.shape[0]

    def summed(cols):
        return jnp.concatenate([top_ref[:, cols], low_ref[:, cols]], axis=0)

    lane_group = lax.broadcasted_iota(jnp.int32, (count, 128), 1) // TAIL
    for j in range(5):
        for h in range(HEADS):
            group = group_ref[h * count : (h + 1) * count, :]
            if j < 4:
                value = jnp.where(group == j, summed(slice(h * MAIN, (h + 1) * MAIN)), 0.0)
            else:
                at = HEADS * MAIN + h * TAIL
                tail = summed(slice(at, at + TAIL))
                tail = jnp.concatenate([tail] * 4, axis=1)
                value = jnp.where(group == lane_group.astype(F32), tail, 0.0)
            top = value.astype(BF16)
            rows[j, h * count : (h + 1) * count, :MAIN] = top
            rows[j, h * count : (h + 1) * count, MAIN:] = (value - top.astype(F32)).astype(BF16)
        found = jnp.dot(select_ref[...], rows[j], preferred_element_type=F32)
        found = found[:, :MAIN] + found[:, MAIN:]
        for k in range(GROUP):
            out_ref[pl.ds(j * GROUP + k, 128, stride=CHUNK), :] = found[k * 128 : (k + 1) * 128]
    out_ref[pl.ds(CAP + GROUP, 128, stride=CHUNK), :] = sent_ref[...]


def update_kernel(got_ref, table_ref, sums_ref, new_table_ref, new_sum_ref, values, select):
    owned = table_ref.shape[1]
    slots = got_ref[pl.ds(CAP + GROUP, 128, stride=CHUNK), :]
    ids = (lax.broadcasted_iota(jnp.int32, (128, owned), 1) + 1).astype(F32)
    for k in range(CAP):
        at = slice(k * 128, (k + 1) * 128)
        select[at, :] = jnp.where(slots[:, k : k + 1] == ids, 1.0, 0.0).astype(BF16)
        main = got_ref[pl.ds(k, 128, stride=CHUNK), :].T
        top = main.astype(BF16)
        values[:MAIN, at] = top
        values[EH : EH + MAIN, at] = (main - top.astype(F32)).astype(BF16)
    for k in range(GROUP):
        tail = got_ref[pl.ds(CAP + k, 128, stride=CHUNK), :].T
        top = tail.astype(BF16)
        rest = (tail - top.astype(F32)).astype(BF16)
        for j in range(4):
            at = slice((j * GROUP + k) * 128, (j * GROUP + k + 1) * 128)
            values[MAIN:EH, at] = top[j * TAIL : (j + 1) * TAIL]
            values[EH + MAIN :, at] = rest[j * TAIL : (j + 1) * TAIL]
    both = jnp.dot(values[...], select[...], preferred_element_type=F32)
    row_sum = both[:EH] + both[EH:]
    new_sum = sums_ref[...] + row_sum * row_sum
    new_sum_ref[...] = new_sum
    new_table_ref[...] = table_ref[...] - LEARN_RATE * row_sum / (jnp.sqrt(new_sum) + EPSILON)


def whole(shape):
    return pl.BlockSpec(shape, lambda *_: (0,) * len(shape))


def body(hidden, out_grad, memory, w_key, w_value, row_owner, row_slot, mem_table, adagrad_sum):
    tokens, width = hidden.shape
    depth = memory.shape[1]
    quarter = tokens // 4
    tile = 256
    tiles = tokens // tile

    position = lax.axis_index("dp").astype(jnp.int32)
    core = position & 1
    place = jnp.stack([position >> 3, (position >> 1) & 3, core])
    at = jnp.stack([lax.axis_index("tensor").astype(jnp.int32), core])

    def quarter_at(p, s):
        return (s[0] + 4 + (1 + p) * (2 * s[1] - 1)) & 3

    start = quarter_at(0, at).reshape(1)

    def by_rows(cols):
        return pl.BlockSpec((tile, cols), lambda i, s: (i, 0))

    chunk = whole((quarter, 2 * width))
    part, first_both = pl.pallas_call(
        forward_kernel,
        grid_spec=pltpu.PrefetchScalarGridSpec(
            num_scalar_prefetch=1,
            grid=(tiles,),
            in_specs=[
                by_rows(depth),
                by_rows(width),
                by_rows(width),
                whole((depth, width)),
                whole((depth, width)),
            ],
            out_specs=[
                pl.BlockSpec((2, tile), lambda i, s: (0, i)),
                chunk,
            ],
        ),
        out_shape=[
            jax.ShapeDtypeStruct((2, tokens), F32),
            jax.ShapeDtypeStruct((quarter, 2 * width), BF16),
        ],
        compiler_params=params(53),
        cost_estimate=cost(4 * tokens * depth * width, 12 << 20),
        name="forward",
    )(start, memory, hidden, out_grad, w_key, w_value)
    parts = [part] + [
        lax.ppermute(part, "tensor", [(i, (i + step) % 4) for i in range(4)]) for step in (1, 2, 3)
    ]

    def swapped(value, bits):
        def goal(i):
            dp, tensor = i // 4, i % 4
            by = bits[dp % 2]
            return (dp ^ by[0]) * 4 + (tensor ^ by[1])

        return lax.ppermute(value, ("dp", "tensor"), [(i, goal(i)) for i in range(128)])

    def turned(value):
        def goal(i):
            return i // 4 * 4 + (i + (1, 3)[i // 4 % 2]) % 4

        return lax.ppermute(value, ("dp", "tensor"), [(i, goal(i)) for i in range(128)])

    def tile_spec(cols):
        return pl.BlockSpec((quarter, cols), lambda p, s: (quarter_at(p, s), 0))

    weights = [whole((depth, width))] * 2
    part_whole = whole((2, tokens))
    top = 144
    low = quarter - top

    first_top, first_low = pl.pallas_call(
        first_kernel,
        grid_spec=pltpu.PrefetchScalarGridSpec(
            num_scalar_prefetch=1,
            grid=(1,),
            in_specs=[part_whole] * 4 + [chunk] + weights,
            out_specs=[whole((top, depth)), whole((low, depth))],
        ),
        out_shape=[
            jax.ShapeDtypeStruct((top, depth), F32),
            jax.ShapeDtypeStruct((low, depth), F32),
        ],
        compiler_params=params(20),
        cost_estimate=cost(4 * quarter * depth * width, 6 << 20),
        name="first",
    )(start, *parts, first_both, w_key, w_value)
    parts, _ = lax.optimization_barrier((parts, first_low))

    def by_rows(cols):
        return pl.BlockSpec((quarter, cols), lambda i: (i, 0))

    total_spec = pl.BlockSpec((2, quarter), lambda i: (0, i))
    both = pl.pallas_call(
        gate_kernel,
        grid=(4,),
        in_specs=[total_spec] * 4 + [by_rows(width)] * 2,
        out_specs=by_rows(2 * width),
        out_shape=jax.ShapeDtypeStruct((tokens, 2 * width), BF16),
        compiler_params=params(24),
        cost_estimate=cost(1, 1),
        name="gate",
    )(*parts, hidden, out_grad)

    grad_spec = whole((depth // 2, 2 * width))
    mine, other = pl.pallas_call(
        weight_grad_kernel,
        grid_spec=pltpu.PrefetchScalarGridSpec(
            num_scalar_prefetch=1,
            grid=(2,),
            in_specs=[
                pl.BlockSpec((tokens, depth // 2), lambda i, s: (0, i)),
                whole((tokens, 2 * width)),
            ],
            out_specs=[grad_spec, grad_spec],
        ),
        out_shape=[jax.ShapeDtypeStruct((depth // 2, 2 * width), F32)] * 2,
        compiler_params=params(32),
        cost_estimate=cost(1, 1),
        name="weight_grad",
    )(place, memory, both)
    late, _ = lax.optimization_barrier((both, other))
    rest_top, rest_low = pl.pallas_call(
        rest_kernel,
        grid_spec=pltpu.PrefetchScalarGridSpec(
            num_scalar_prefetch=1,
            grid=(3,),
            in_specs=[
                pl.BlockSpec((quarter, 2 * width), lambda p, s: (quarter_at(p + 1, s), 0)),
                *weights,
            ],
            out_specs=[
                pl.BlockSpec((1, top, depth), lambda p, s: (p, 0, 0)),
                pl.BlockSpec((1, low, depth), lambda p, s: (p, 0, 0)),
            ],
        ),
        out_shape=[
            jax.ShapeDtypeStruct((3, top, depth), F32),
            jax.ShapeDtypeStruct((3, low, depth), F32),
        ],
        compiler_params=params(24),
        cost_estimate=cost(1, 1),
        name="rest",
    )(at, late, w_key, w_value)

    def folded(value, bits):
        half = value.shape[0] // 2
        return value[:half] + swapped(value[half:], bits)

    moved_top = turned(first_top) + rest_top[0]
    moved_low = turned(first_low) + rest_low[0]
    moved_top, moved_low, owners, slots = lax.optimization_barrier(
        (moved_top, moved_low, row_owner.T, row_slot.T)
    )
    passed_top = turned(moved_top)
    passed_low = turned(moved_low)
    select, group, sent = pl.pallas_call(
        ranks_kernel,
        grid_spec=pltpu.PrefetchScalarGridSpec(
            num_scalar_prefetch=1,
            grid=(1,),
            in_specs=[pl.BlockSpec((HEADS, quarter), lambda i, s: (0, s[0]))] * 2,
            out_specs=[
                whole((GROUP * 128, HEADS * quarter)),
                whole((HEADS * quarter, 128)),
                whole((128, 128)),
            ],
        ),
        out_shape=[
            jax.ShapeDtypeStruct((GROUP * 128, HEADS * quarter), BF16),
            jax.ShapeDtypeStruct((HEADS * quarter, 128), F32),
            jax.ShapeDtypeStruct((128, 128), F32),
        ],
        compiler_params=params(32),
        cost_estimate=cost(1 << 36, 1 << 27),
        name="ranks",
    )(at, owners, slots)
    mine, select = lax.optimization_barrier((mine, select))
    pair = mine + swapped(other, ((1, 0), (1, 0)))
    rest_top, rest_low, pair = lax.optimization_barrier((rest_top, rest_low, pair))
    moved_top = turned(passed_top + rest_top[1])
    moved_low = turned(passed_low + rest_low[1])
    grads = folded(pair, ((8, 0), (2, 0)))
    rest_top, rest_low, grads = lax.optimization_barrier((rest_top, rest_low, grads))
    sum_top = moved_top + rest_top[2]
    sum_low = moved_low + rest_low[2]
    grads = folded(grads, ((24, 0), (6, 0)))

    packed = pl.pallas_call(
        pack_kernel,
        grid=(1,),
        in_specs=[
            whole((top, depth)),
            whole((low, depth)),
            whole((GROUP * 128, HEADS * quarter)),
            whole((HEADS * quarter, 128)),
            whole((128, 128)),
        ],
        out_specs=whole((128 * CHUNK, 128)),
        out_shape=jax.ShapeDtypeStruct((128 * CHUNK, 128), F32),
        scratch_shapes=[pltpu.VMEM((5, HEADS * quarter, 256), BF16)],
        compiler_params=params(32),
        cost_estimate=cost(2 * 1024 * 2048 * 1280, 12 << 20),
        name="pack",
    )(sum_top, sum_low, select, group, sent)
    packed, grads, parts = lax.optimization_barrier((packed, grads, parts))
    hidden_grad = pl.pallas_call(
        hidden_grad_kernel,
        grid=(4,),
        in_specs=[total_spec] * 4 + [by_rows(depth), whole((depth, width))],
        out_specs=by_rows(width),
        out_shape=jax.ShapeDtypeStruct((tokens, width), BF16),
        compiler_params=params(58),
        cost_estimate=cost(2 * tokens * depth * width, 6 << 20),
        name="hidden_grad",
    )(*parts, memory, w_key)
    received = lax.all_to_all(
        packed.reshape(128, 1, CHUNK * 128),
        ("dp", "tensor"),
        split_axis=0,
        concat_axis=0,
        tiled=True,
    ).reshape(128 * CHUNK, 128)
    blocks = grads.reshape(4, -1, 2 * width)
    got = [
        swapped(blocks[i], ((2 * bits, 0), (8 * bits, 0))) for i, bits in ((1, 3), (2, 1), (3, 2))
    ]
    received, hidden_grad = lax.optimization_barrier((received, hidden_grad))
    owned = mem_table.shape[0]
    table_spec = whole((EH, owned))
    new_table, new_sum = pl.pallas_call(
        update_kernel,
        grid=(1,),
        in_specs=[whole((128 * CHUNK, 128)), table_spec, table_spec],
        out_specs=[table_spec, table_spec],
        out_shape=[jax.ShapeDtypeStruct((EH, owned), F32)] * 2,
        scratch_shapes=[
            pltpu.VMEM((2 * EH, CAP * 128), BF16),
            pltpu.VMEM((CAP * 128, owned), BF16),
        ],
        compiler_params=params(48),
        cost_estimate=cost(4 * EH * 4096 * 512, 5 << 20),
        name="update",
    )(received, mem_table.T, adagrad_sum.T)
    kept, new_table = lax.optimization_barrier((blocks[0], new_table))
    total = (kept + got[0]) + (got[1] + got[2])
    key_weight_grad = total[:, :width]
    value_weight_grad = total[:, width:]
    return (hidden_grad, key_weight_grad, value_weight_grad, new_table.T, new_sum.T)


def solution(mesh):
    return jax.shard_map(
        body,
        mesh=mesh,
        in_specs=(
            P("dp", "tensor"),
            P("dp", "tensor"),
            P("dp", None),
            P(None, "tensor"),
            P(None, "tensor"),
            P("dp", None),
            P("dp", None),
            P(("dp", "tensor"), None),
            P(("dp", "tensor"), None),
        ),
        out_specs=(
            P("dp", "tensor"),
            P("dp", "tensor"),
            P("dp", "tensor"),
            P(("dp", "tensor"), None),
            P(("dp", "tensor"), None),
        ),
        check_vma=False,
    )
```

```python
import functools

import jax
import jax.numpy as jnp
from jax import lax
from jax.experimental import pallas as pl
from jax.experimental.pallas import tpu as pltpu
from jax.sharding import PartitionSpec as P

D = 2560
HEADS = 8
EH = 160
MAIN = 128
TAIL = EH - MAIN
CAP = 32
GROUP = CAP // 4
CHUNK = CAP + GROUP + 1
LEARN_RATE = 0.5
EPSILON = 1e-06
F32 = jnp.float32
BF16 = jnp.bfloat16
OVER_ROWS = (((0,), (0,)), ((), ()))
OVER_LANES = (((1,), (1,)), ((), ()))


def params(mib):
    return pltpu.CompilerParams(vmem_limit_bytes=mib << 20)


def cost(flops, moved):
    return pl.CostEstimate(flops=flops, bytes_accessed=moved, transcendentals=0)


def row_sums(x):
    lanes = x[:, :128]
    for at in range(128, x.shape[1], 128):
        lanes = lanes + x[:, at : at + 128]
    return jnp.sum(lanes.T, axis=0, keepdims=True)


def as_columns(row, width):
    column = jnp.broadcast_to(row, (128, row.shape[1])).T
    return jnp.concatenate([column] * (width // 128), axis=1)


def ranks_kernel(at_ref, owners_ref, slots_ref, select_ref, group_ref, sent_ref):
    count = owners_ref.shape[1]
    owners = owners_ref[...]
    slot_plus = slots_ref[...] + 1
    ids = lax.broadcasted_iota(jnp.int32, (128, count), 0)
    hits = jnp.zeros((128, count), F32)
    for h in range(HEADS):
        hits = hits + jnp.where(owners[h : h + 1] == ids, 1.0, 0.0)
    earlier = lax.broadcasted_iota(jnp.int32, (count, count), 0) < lax.broadcasted_iota(
        jnp.int32, (count, count), 1
    )
    before = jnp.dot(
        hits.astype(BF16), jnp.where(earlier, 1.0, 0.0).astype(BF16), preferred_element_type=F32
    )
    high = jnp.zeros((128, 128), F32)
    low = jnp.zeros((128, 128), F32)
    for h in range(HEADS):
        match = owners[h : h + 1] == ids
        rank = jnp.sum(jnp.where(match, before, 0.0), axis=0, keepdims=True).astype(jnp.int32)
        place = jnp.where(rank == ids, 1.0, 0.0).astype(BF16)
        slot = slot_plus[h : h + 1]
        upper = jnp.where(match, (slot // 16).astype(F32), 0.0).astype(BF16)
        lower = jnp.where(match, (slot % 16).astype(F32), 0.0).astype(BF16)
        high = high + lax.dot_general(upper, place, OVER_LANES, preferred_element_type=F32)
        low = low + lax.dot_general(lower, place, OVER_LANES, preferred_element_type=F32)
        groups = jnp.broadcast_to((rank // GROUP).astype(F32), (128, count)).T
        within = jnp.where(match, rank % GROUP, -1)
        for piece in range(2):
            tokens = slice(piece * 128, (piece + 1) * 128)
            columns = slice((piece * HEADS + h) * 128, (piece * HEADS + h + 1) * 128)
            group_ref[columns, :] = groups[tokens]
            for k in range(GROUP):
                select_ref[k * 128 : (k + 1) * 128, columns] = jnp.where(
                    within[:, tokens] == k, 1.0, 0.0
                ).astype(BF16)
    sent_ref[...] = 16.0 * high + low


def forward_kernel(
    at_ref, memory_ref, hidden_ref, grad_ref, wk_ref, wv_ref, part_ref, first_ref
):
    @pl.when(pl.program_id(0) == at_ref[0])
    def _():
        width = hidden_ref.shape[1]
        first_ref[:, :width] = hidden_ref[...]
        first_ref[:, width:] = grad_ref[...]

    memory = memory_ref[...]
    proj_key = jnp.dot(memory, wk_ref[...], preferred_element_type=F32)
    part_ref[0:1, :] = row_sums(hidden_ref[...].astype(F32) * proj_key)
    proj_value = jnp.dot(memory, wv_ref[...], preferred_element_type=F32)
    part_ref[1:2, :] = row_sums(grad_ref[...].astype(F32) * proj_value)


def gate_columns(total, width):
    root = jnp.sqrt(jnp.full((1, 1), D, F32))
    gate = jax.nn.sigmoid(total[0:1] / root)
    score = total[1:2] * gate * (1.0 - gate) / root
    return as_columns(gate, width), as_columns(score, width)


def summed_parts(part_refs, at=slice(None)):
    p0, p1, p2, p3 = (ref[:, at] for ref in part_refs)
    return (p0 + p1) + (p2 + p3)


def memory_grad_tile(key_grad, value_grad, wk_ref, wv_ref, *out_refs):
    grads = lax.dot_general(
        key_grad, wk_ref[...], OVER_LANES, preferred_element_type=F32
    ) + lax.dot_general(value_grad, wv_ref[...], OVER_LANES, preferred_element_type=F32)
    at = 0
    for out_ref in out_refs:
        here = grads[at : at + out_ref.shape[0]]
        for h in range(HEADS):
            first = h * EH
            out_ref[:, h * MAIN : (h + 1) * MAIN] = here[:, first : first + MAIN]
            tail = slice(HEADS * MAIN + h * TAIL, HEADS * MAIN + (h + 1) * TAIL)
            out_ref[:, tail] = here[:, first + MAIN : first + EH]
        at += out_ref.shape[0]


def first_kernel(at_ref, p0, p1, p2, p3, first_ref, wk_ref, wv_ref, top_ref, low_ref):
    count, width = first_ref.shape[0], first_ref.shape[1] // 2
    tile = pl.ds(pl.multiple_of(at_ref[0] * count, count), count)
    gates, scores = gate_columns(summed_parts((p0, p1, p2, p3), tile), width)
    key_grad = (scores * first_ref[:, :width].astype(F32)).astype(BF16)
    value_grad = (gates * first_ref[:, width:].astype(F32)).astype(BF16)
    memory_grad_tile(key_grad, value_grad, wk_ref, wv_ref, top_ref, low_ref)


def gate_kernel(p0, p1, p2, p3, hidden_ref, grad_ref, both_ref):
    width = hidden_ref.shape[1]
    gates, scores = gate_columns(summed_parts((p0, p1, p2, p3)), width)
    both_ref[:, :width] = (scores * hidden_ref[...].astype(F32)).astype(BF16)
    both_ref[:, width:] = (gates * grad_ref[...].astype(F32)).astype(BF16)


def hidden_grad_kernel(p0, p1, p2, p3, memory_ref, wk_ref, out_ref):
    _, scores = gate_columns(summed_parts((p0, p1, p2, p3)), out_ref.shape[1])
    proj_key = jnp.dot(memory_ref[...], wk_ref[...], preferred_element_type=F32)
    out_ref[...] = (scores * proj_key).astype(BF16)


def rest_kernel(at_ref, both_ref, wk_ref, wv_ref, top_ref, low_ref):
    width = wk_ref.shape[1]
    memory_grad_tile(
        both_ref[:, :width], both_ref[:, width:], wk_ref, wv_ref, top_ref.at[0], low_ref.at[0]
    )


def weight_grad_kernel(at_ref, memory_ref, both_ref, mine_ref, other_ref):
    i = pl.program_id(0)
    block = mine_ref.shape[0] // 16
    rows = memory_ref.shape[1]
    me_x, me_z, me_core = at_ref[0], at_ref[1], at_ref[2]

    def order(r):
        return jnp.where(r == 0, 0, jnp.where(r == 3, 1, r + 1))

    found = lax.dot_general(
        memory_ref[...], both_ref[...], OVER_ROWS, preferred_element_type=F32
    )
    for p in range(rows // block):
        x = order((i * 2 + p // 8) ^ me_x)
        z = order((p % 8 // 2) ^ me_z)
        place = x * 4 + z if p % 2 == 0 else z * 4 + x
        to = pl.ds(pl.multiple_of(place * block, 8), block)
        value = found[p * block : (p + 1) * block]

        @pl.when(me_core == p % 2)
        def _():
            mine_ref[to, :] = value

        @pl.when(me_core != p % 2)
        def _():
            other_ref[to, :] = value


def packed_group(j, sum_ref, select_ref, group_ref, rows):
    count = sum_ref.shape[0]
    lane_group = lax.broadcasted_iota(jnp.int32, (count, 128), 1) // TAIL
    for h in range(HEADS):
        group = group_ref[h * count : (h + 1) * count, :]
        if j < 4:
            value = jnp.where(group == j, sum_ref[:, h * MAIN : (h + 1) * MAIN], 0.0)
        else:
            at = HEADS * MAIN + h * TAIL
            tail = jnp.concatenate([sum_ref[:, at : at + TAIL]] * 4, axis=1)
            value = jnp.where(group == lane_group.astype(F32), tail, 0.0)
        top = value.astype(BF16)
        rows[j, h * count : (h + 1) * count, :MAIN] = top
        rows[j, h * count : (h + 1) * count, MAIN:] = (value - top.astype(F32)).astype(BF16)
    found = jnp.dot(select_ref[...], rows[j], preferred_element_type=F32)
    return found[:, :MAIN] + found[:, MAIN:]


def pack_top_kernel(sum_ref, select_ref, group_ref, out_ref, rows):
    for j in range(5):
        out_ref[j] = packed_group(j, sum_ref, select_ref, group_ref, rows)


def pack_low_kernel(sum_ref, select_ref, group_ref, part_ref, sent_ref, out_ref, rows):
    for j in range(5):
        found = part_ref[j] + packed_group(j, sum_ref, select_ref, group_ref, rows)
        for k in range(GROUP):
            out_ref[pl.ds(j * GROUP + k, 128, stride=CHUNK), :] = found[k * 128 : (k + 1) * 128]
    out_ref[pl.ds(CAP + GROUP, 128, stride=CHUNK), :] = sent_ref[...]


def update_kernel(got_ref, table_ref, sums_ref, new_table_ref, new_sum_ref, values, select):
    owned = table_ref.shape[1]
    slots = got_ref[pl.ds(CAP + GROUP, 128, stride=CHUNK), :]
    ids = (lax.broadcasted_iota(jnp.int32, (128, owned), 1) + 1).astype(F32)
    for k in range(CAP):
        at = slice(k * 128, (k + 1) * 128)
        select[at, :] = jnp.where(slots[:, k : k + 1] == ids, 1.0, 0.0).astype(BF16)
        main = got_ref[pl.ds(k, 128, stride=CHUNK), :].T
        top = main.astype(BF16)
        values[:MAIN, at] = top
        values[EH : EH + MAIN, at] = (main - top.astype(F32)).astype(BF16)
    for k in range(GROUP):
        tail = got_ref[pl.ds(CAP + k, 128, stride=CHUNK), :].T
        top = tail.astype(BF16)
        rest = (tail - top.astype(F32)).astype(BF16)
        for j in range(4):
            at = slice((j * GROUP + k) * 128, (j * GROUP + k + 1) * 128)
            values[MAIN:EH, at] = top[j * TAIL : (j + 1) * TAIL]
            values[EH + MAIN :, at] = rest[j * TAIL : (j + 1) * TAIL]
    both = jnp.dot(values[...], select[...], preferred_element_type=F32)
    row_sum = both[:EH] + both[EH:]
    new_sum = sums_ref[...] + row_sum * row_sum
    new_sum_ref[...] = new_sum
    new_table_ref[...] = table_ref[...] - LEARN_RATE * row_sum / (jnp.sqrt(new_sum) + EPSILON)


def whole(shape):
    return pl.BlockSpec(shape, lambda *_: (0,) * len(shape))


def body(hidden, out_grad, memory, w_key, w_value, row_owner, row_slot, mem_table, adagrad_sum):
    tokens, width = hidden.shape
    depth = memory.shape[1]
    quarter = tokens // 4
    tile = 256
    tiles = tokens // tile

    position = lax.axis_index("dp").astype(jnp.int32)
    core = position & 1
    place = jnp.stack([position >> 3, (position >> 1) & 3, core])
    at = jnp.stack([lax.axis_index("tensor").astype(jnp.int32), core])

    def quarter_at(p, s):
        return (s[0] + 4 + (1 + p) * (2 * s[1] - 1)) & 3

    start = quarter_at(0, at).reshape(1)

    def by_rows(cols):
        return pl.BlockSpec((tile, cols), lambda i, s: (i, 0))

    chunk = whole((quarter, 2 * width))
    part, first_both = pl.pallas_call(
        forward_kernel,
        grid_spec=pltpu.PrefetchScalarGridSpec(
            num_scalar_prefetch=1,
            grid=(tiles,),
            in_specs=[
                by_rows(depth),
                by_rows(width),
                by_rows(width),
                whole((depth, width)),
                whole((depth, width)),
            ],
            out_specs=[
                pl.BlockSpec((2, tile), lambda i, s: (0, i)),
                chunk,
            ],
        ),
        out_shape=[
            jax.ShapeDtypeStruct((2, tokens), F32),
            jax.ShapeDtypeStruct((quarter, 2 * width), BF16),
        ],
        compiler_params=params(53),
        cost_estimate=cost(4 * tokens * depth * width, 12 << 20),
        name="forward",
    )(start, memory, hidden, out_grad, w_key, w_value)
    parts = [part] + [
        lax.ppermute(part, "tensor", [(i, (i + step) % 4) for i in range(4)]) for step in (1, 2, 3)
    ]

    def swapped(value, bits):
        def goal(i):
            dp, tensor = i // 4, i % 4
            by = bits[dp % 2]
            return (dp ^ by[0]) * 4 + (tensor ^ by[1])

        return lax.ppermute(value, ("dp", "tensor"), [(i, goal(i)) for i in range(128)])

    def turned(value):
        def goal(i):
            return i // 4 * 4 + (i + (1, 3)[i // 4 % 2]) % 4

        return lax.ppermute(value, ("dp", "tensor"), [(i, goal(i)) for i in range(128)])

    def tile_spec(cols):
        return pl.BlockSpec((quarter, cols), lambda p, s: (quarter_at(p, s), 0))

    weights = [whole((depth, width))] * 2
    part_whole = whole((2, tokens))
    top = 128
    low = quarter - top

    first_top, first_low = pl.pallas_call(
        first_kernel,
        grid_spec=pltpu.PrefetchScalarGridSpec(
            num_scalar_prefetch=1,
            grid=(1,),
            in_specs=[part_whole] * 4 + [chunk] + weights,
            out_specs=[whole((top, depth)), whole((low, depth))],
        ),
        out_shape=[
            jax.ShapeDtypeStruct((top, depth), F32),
            jax.ShapeDtypeStruct((low, depth), F32),
        ],
        compiler_params=params(20),
        cost_estimate=cost(4 * quarter * depth * width, 6 << 20),
        name="first",
    )(start, *parts, first_both, w_key, w_value)
    parts, _ = lax.optimization_barrier((parts, first_low))

    def by_rows(cols):
        return pl.BlockSpec((quarter, cols), lambda i: (i, 0))

    total_spec = pl.BlockSpec((2, quarter), lambda i: (0, i))
    both = pl.pallas_call(
        gate_kernel,
        grid=(4,),
        in_specs=[total_spec] * 4 + [by_rows(width)] * 2,
        out_specs=by_rows(2 * width),
        out_shape=jax.ShapeDtypeStruct((tokens, 2 * width), BF16),
        compiler_params=params(24),
        cost_estimate=cost(1, 1),
        name="gate",
    )(*parts, hidden, out_grad)

    grad_spec = whole((depth // 2, 2 * width))
    mine, other = pl.pallas_call(
        weight_grad_kernel,
        grid_spec=pltpu.PrefetchScalarGridSpec(
            num_scalar_prefetch=1,
            grid=(2,),
            in_specs=[
                pl.BlockSpec((tokens, depth // 2), lambda i, s: (0, i)),
                whole((tokens, 2 * width)),
            ],
            out_specs=[grad_spec, grad_spec],
        ),
        out_shape=[jax.ShapeDtypeStruct((depth // 2, 2 * width), F32)] * 2,
        compiler_params=params(32),
        cost_estimate=cost(1, 1),
        name="weight_grad",
    )(place, memory, both)
    late, _ = lax.optimization_barrier((both, other))
    rest_top, rest_low = pl.pallas_call(
        rest_kernel,
        grid_spec=pltpu.PrefetchScalarGridSpec(
            num_scalar_prefetch=1,
            grid=(3,),
            in_specs=[
                pl.BlockSpec((quarter, 2 * width), lambda p, s: (quarter_at(p + 1, s), 0)),
                *weights,
            ],
            out_specs=[
                pl.BlockSpec((1, top, depth), lambda p, s: (p, 0, 0)),
                pl.BlockSpec((1, low, depth), lambda p, s: (p, 0, 0)),
            ],
        ),
        out_shape=[
            jax.ShapeDtypeStruct((3, top, depth), F32),
            jax.ShapeDtypeStruct((3, low, depth), F32),
        ],
        compiler_params=params(24),
        cost_estimate=cost(1, 1),
        name="rest",
    )(at, late, w_key, w_value)

    def folded(value, bits):
        half = value.shape[0] // 2
        return value[:half] + swapped(value[half:], bits)

    moved_top = turned(first_top) + rest_top[0]
    moved_low = turned(first_low) + rest_low[0]
    moved_top, moved_low, owners, slots = lax.optimization_barrier(
        (moved_top, moved_low, row_owner.T, row_slot.T)
    )
    passed_top = turned(moved_top)
    passed_low = turned(moved_low)
    select, group, sent = pl.pallas_call(
        ranks_kernel,
        grid_spec=pltpu.PrefetchScalarGridSpec(
            num_scalar_prefetch=1,
            grid=(1,),
            in_specs=[pl.BlockSpec((HEADS, quarter), lambda i, s: (0, s[0]))] * 2,
            out_specs=[
                whole((GROUP * 128, HEADS * quarter)),
                whole((HEADS * quarter, 128)),
                whole((128, 128)),
            ],
        ),
        out_shape=[
            jax.ShapeDtypeStruct((GROUP * 128, HEADS * quarter), BF16),
            jax.ShapeDtypeStruct((HEADS * quarter, 128), F32),
            jax.ShapeDtypeStruct((128, 128), F32),
        ],
        compiler_params=params(32),
        cost_estimate=cost(1 << 36, 1 << 27),
        name="ranks",
    )(at, owners, slots)
    mine, select = lax.optimization_barrier((mine, select))
    pair = mine + swapped(other, ((1, 0), (1, 0)))
    rest_top, rest_low, pair = lax.optimization_barrier((rest_top, rest_low, pair))
    moved_top = turned(passed_top + rest_top[1])
    moved_low = turned(passed_low + rest_low[1])
    grads = folded(pair, ((8, 0), (2, 0)))
    rest_top, rest_low, grads = lax.optimization_barrier((rest_top, rest_low, grads))
    sum_top = moved_top + rest_top[2]
    sum_low = moved_low + rest_low[2]
    grads = folded(grads, ((24, 0), (6, 0)))

    half_rows = HEADS * quarter // 2

    def piece_specs(piece):
        return [
            whole((quarter // 2, depth)),
            pl.BlockSpec((GROUP * 128, half_rows), lambda i: (0, piece)),
            pl.BlockSpec((half_rows, 128), lambda i: (piece, 0)),
        ]

    pack_part = pl.pallas_call(
        pack_top_kernel,
        grid=(1,),
        in_specs=piece_specs(0),
        out_specs=whole((5, GROUP * 128, 128)),
        out_shape=jax.ShapeDtypeStruct((5, GROUP * 128, 128), F32),
        scratch_shapes=[pltpu.VMEM((5, half_rows, 256), BF16)],
        compiler_params=params(24),
        cost_estimate=cost(1024 * 2048 * 1280, 8 << 20),
        name="pack_top",
    )(sum_top, select, group)
    packed = pl.pallas_call(
        pack_low_kernel,
        grid=(1,),
        in_specs=[
            *piece_specs(1),
            whole((5, GROUP * 128, 128)),
            whole((128, 128)),
        ],
        out_specs=whole((128 * CHUNK, 128)),
        out_shape=jax.ShapeDtypeStruct((128 * CHUNK, 128), F32),
        scratch_shapes=[pltpu.VMEM((5, half_rows, 256), BF16)],
        compiler_params=params(32),
        cost_estimate=cost(1024 * 2048 * 1280, 12 << 20),
        name="pack_low",
    )(sum_low, select, group, pack_part, sent)
    packed, grads, parts = lax.optimization_barrier((packed, grads, parts))
    hidden_grad = pl.pallas_call(
        hidden_grad_kernel,
        grid=(4,),
        in_specs=[total_spec] * 4 + [by_rows(depth), whole((depth, width))],
        out_specs=by_rows(width),
        out_shape=jax.ShapeDtypeStruct((tokens, width), BF16),
        compiler_params=params(58),
        cost_estimate=cost(2 * tokens * depth * width, 6 << 20),
        name="hidden_grad",
    )(*parts, memory, w_key)
    received = lax.all_to_all(
        packed.reshape(128, 1, CHUNK * 128),
        ("dp", "tensor"),
        split_axis=0,
        concat_axis=0,
        tiled=True,
    ).reshape(128 * CHUNK, 128)
    blocks = grads.reshape(4, -1, 2 * width)
    got = [
        swapped(blocks[i], ((2 * bits, 0), (8 * bits, 0))) for i, bits in ((1, 3), (2, 1), (3, 2))
    ]
    received, hidden_grad = lax.optimization_barrier((received, hidden_grad))
    owned = mem_table.shape[0]
    table_spec = whole((EH, owned))
    new_table, new_sum = pl.pallas_call(
        update_kernel,
        grid=(1,),
        in_specs=[whole((128 * CHUNK, 128)), table_spec, table_spec],
        out_specs=[table_spec, table_spec],
        out_shape=[jax.ShapeDtypeStruct((EH, owned), F32)] * 2,
        scratch_shapes=[
            pltpu.VMEM((2 * EH, CAP * 128), BF16),
            pltpu.VMEM((CAP * 128, owned), BF16),
        ],
        compiler_params=params(48),
        cost_estimate=cost(4 * EH * 4096 * 512, 5 << 20),
        name="update",
    )(received, mem_table.T, adagrad_sum.T)
    kept, new_table = lax.optimization_barrier((blocks[0], new_table))
    sides = [slice(0, width), slice(width, 2 * width)]
    key_weight_grad, value_weight_grad = (
        (kept[:, at] + got[0][:, at]) + (got[1][:, at] + got[2][:, at]) for at in sides
    )
    return (hidden_grad, key_weight_grad, value_weight_grad, new_table.T, new_sum.T)


def solution(mesh):
    return jax.shard_map(
        body,
        mesh=mesh,
        in_specs=(
            P("dp", "tensor"),
            P("dp", "tensor"),
            P("dp", None),
            P(None, "tensor"),
            P(None, "tensor"),
            P("dp", None),
            P("dp", None),
            P(("dp", "tensor"), None),
            P(("dp", "tensor"), None),
        ),
        out_specs=(
            P("dp", "tensor"),
            P("dp", "tensor"),
            P("dp", "tensor"),
            P(("dp", "tensor"), None),
            P(("dp", "tensor"), None),
        ),
        check_vma=False,
    )
```

```python
import functools

import jax
import jax.numpy as jnp
from jax import lax
from jax.experimental import pallas as pl
from jax.experimental.pallas import tpu as pltpu
from jax.sharding import PartitionSpec as P

D = 2560
HEADS = 8
EH = 160
MAIN = 128
TAIL = EH - MAIN
CAP = 32
GROUP = CAP // 4
CHUNK = CAP + GROUP + 1
LEARN_RATE = 0.5
EPSILON = 1e-06
F32 = jnp.float32
BF16 = jnp.bfloat16
OVER_ROWS = (((0,), (0,)), ((), ()))
OVER_LANES = (((1,), (1,)), ((), ()))


def params(mib):
    return pltpu.CompilerParams(vmem_limit_bytes=mib << 20)


def cost(flops, moved):
    return pl.CostEstimate(flops=flops, bytes_accessed=moved, transcendentals=0)


def row_sums(x):
    lanes = x[:, :128]
    for at in range(128, x.shape[1], 128):
        lanes = lanes + x[:, at : at + 128]
    return jnp.sum(lanes.T, axis=0, keepdims=True)


def as_columns(row, width):
    column = jnp.broadcast_to(row, (128, row.shape[1])).T
    return jnp.concatenate([column] * (width // 128), axis=1)


def ranks_kernel(at_ref, owners_ref, slots_ref, select_ref, group_ref, sent_ref):
    count = owners_ref.shape[1]
    owners = owners_ref[...]
    slot_plus = slots_ref[...] + 1
    ids = lax.broadcasted_iota(jnp.int32, (128, count), 0)
    hits = jnp.zeros((128, count), F32)
    for h in range(HEADS):
        hits = hits + jnp.where(owners[h : h + 1] == ids, 1.0, 0.0)
    earlier = lax.broadcasted_iota(jnp.int32, (count, count), 0) < lax.broadcasted_iota(
        jnp.int32, (count, count), 1
    )
    before = jnp.dot(
        hits.astype(BF16), jnp.where(earlier, 1.0, 0.0).astype(BF16), preferred_element_type=F32
    )
    high = jnp.zeros((128, 128), F32)
    low = jnp.zeros((128, 128), F32)
    for h in range(HEADS):
        match = owners[h : h + 1] == ids
        rank = jnp.sum(jnp.where(match, before, 0.0), axis=0, keepdims=True).astype(jnp.int32)
        place = jnp.where(rank == ids, 1.0, 0.0).astype(BF16)
        slot = slot_plus[h : h + 1]
        upper = jnp.where(match, (slot // 16).astype(F32), 0.0).astype(BF16)
        lower = jnp.where(match, (slot % 16).astype(F32), 0.0).astype(BF16)
        high = high + lax.dot_general(upper, place, OVER_LANES, preferred_element_type=F32)
        low = low + lax.dot_general(lower, place, OVER_LANES, preferred_element_type=F32)
        groups = jnp.broadcast_to((rank // GROUP).astype(F32), (128, count)).T
        within = jnp.where(match, rank % GROUP, -1)
        for piece in range(2):
            tokens = slice(piece * 128, (piece + 1) * 128)
            columns = slice((piece * HEADS + h) * 128, (piece * HEADS + h + 1) * 128)
            group_ref[columns, :] = groups[tokens]
            for k in range(GROUP):
                select_ref[k * 128 : (k + 1) * 128, columns] = jnp.where(
                    within[:, tokens] == k, 1.0, 0.0
                ).astype(BF16)
    sent_ref[...] = 16.0 * high + low


def forward_kernel(
    at_ref, memory_ref, hidden_ref, grad_ref, wk_ref, wv_ref, part_ref, first_ref
):
    @pl.when(pl.program_id(0) == at_ref[0])
    def _():
        width = hidden_ref.shape[1]
        first_ref[:, :width] = hidden_ref[...]
        first_ref[:, width:] = grad_ref[...]

    memory = memory_ref[...]
    proj_key = jnp.dot(memory, wk_ref[...], preferred_element_type=F32)
    part_ref[0:1, :] = row_sums(hidden_ref[...].astype(F32) * proj_key)
    proj_value = jnp.dot(memory, wv_ref[...], preferred_element_type=F32)
    part_ref[1:2, :] = row_sums(grad_ref[...].astype(F32) * proj_value)


def gate_columns(total, width):
    root = jnp.sqrt(jnp.full((1, 1), D, F32))
    gate = jax.nn.sigmoid(total[0:1] / root)
    score = total[1:2] * gate * (1.0 - gate) / root
    return as_columns(gate, width), as_columns(score, width)


def summed_parts(part_refs, at=slice(None)):
    p0, p1, p2, p3 = (ref[:, at] for ref in part_refs)
    return (p0 + p1) + (p2 + p3)


def memory_grad_tile(key_grad, value_grad, wk_ref, wv_ref, *out_refs):
    grads = lax.dot_general(
        key_grad, wk_ref[...], OVER_LANES, preferred_element_type=F32
    ) + lax.dot_general(value_grad, wv_ref[...], OVER_LANES, preferred_element_type=F32)
    at = 0
    for out_ref in out_refs:
        here = grads[at : at + out_ref.shape[0]]
        for h in range(HEADS):
            first = h * EH
            out_ref[:, h * MAIN : (h + 1) * MAIN] = here[:, first : first + MAIN]
            tail = slice(HEADS * MAIN + h * TAIL, HEADS * MAIN + (h + 1) * TAIL)
            out_ref[:, tail] = here[:, first + MAIN : first + EH]
        at += out_ref.shape[0]


def first_kernel(at_ref, p0, p1, p2, p3, first_ref, wk_ref, wv_ref, top_ref, low_ref):
    count, width = first_ref.shape[0], first_ref.shape[1] // 2
    tile = pl.ds(pl.multiple_of(at_ref[0] * count, count), count)
    gates, scores = gate_columns(summed_parts((p0, p1, p2, p3), tile), width)
    key_grad = (scores * first_ref[:, :width].astype(F32)).astype(BF16)
    value_grad = (gates * first_ref[:, width:].astype(F32)).astype(BF16)
    memory_grad_tile(key_grad, value_grad, wk_ref, wv_ref, top_ref, low_ref)


def gate_kernel(p0, p1, p2, p3, hidden_ref, grad_ref, both_ref):
    width = hidden_ref.shape[1]
    gates, scores = gate_columns(summed_parts((p0, p1, p2, p3)), width)
    both_ref[:, :width] = (scores * hidden_ref[...].astype(F32)).astype(BF16)
    both_ref[:, width:] = (gates * grad_ref[...].astype(F32)).astype(BF16)


def hidden_grad_kernel(p0, p1, p2, p3, memory_ref, wk_ref, out_ref):
    _, scores = gate_columns(summed_parts((p0, p1, p2, p3)), out_ref.shape[1])
    proj_key = jnp.dot(memory_ref[...], wk_ref[...], preferred_element_type=F32)
    out_ref[...] = (scores * proj_key).astype(BF16)


def rest_kernel(at_ref, both_ref, wk_ref, wv_ref, top_ref, low_ref):
    width = wk_ref.shape[1]
    memory_grad_tile(
        both_ref[:, :width], both_ref[:, width:], wk_ref, wv_ref, top_ref.at[0], low_ref.at[0]
    )


def weight_grad_kernel(at_ref, memory_ref, both_ref, mine_ref, other_ref):
    i = pl.program_id(0)
    block = mine_ref.shape[0] // 16
    rows = memory_ref.shape[1]
    me_x, me_z, me_core = at_ref[0], at_ref[1], at_ref[2]

    def order(r):
        return jnp.where(r == 0, 0, jnp.where(r == 3, 1, r + 1))

    found = lax.dot_general(
        memory_ref[...], both_ref[...], OVER_ROWS, preferred_element_type=F32
    )
    for p in range(rows // block):
        x = order((i * 2 + p // 8) ^ me_x)
        z = order((p % 8 // 2) ^ me_z)
        place = x * 4 + z if p % 2 == 0 else z * 4 + x
        to = pl.ds(pl.multiple_of(place * block, 8), block)
        value = found[p * block : (p + 1) * block]

        @pl.when(me_core == p % 2)
        def _():
            mine_ref[to, :] = value

        @pl.when(me_core != p % 2)
        def _():
            other_ref[to, :] = value


def packed_group(j, sum_ref, select_ref, group_ref, rows):
    count = sum_ref.shape[0]
    lane_group = lax.broadcasted_iota(jnp.int32, (count, 128), 1) // TAIL
    for h in range(HEADS):
        group = group_ref[h * count : (h + 1) * count, :]
        if j < 4:
            value = jnp.where(group == j, sum_ref[:, h * MAIN : (h + 1) * MAIN], 0.0)
        else:
            at = HEADS * MAIN + h * TAIL
            tail = jnp.concatenate([sum_ref[:, at : at + TAIL]] * 4, axis=1)
            value = jnp.where(group == lane_group.astype(F32), tail, 0.0)
        top = value.astype(BF16)
        rows[j, h * count : (h + 1) * count, :MAIN] = top
        rows[j, h * count : (h + 1) * count, MAIN:] = (value - top.astype(F32)).astype(BF16)
    found = jnp.dot(select_ref[...], rows[j], preferred_element_type=F32)
    return found[:, :MAIN] + found[:, MAIN:]


def pack_top_kernel(sum_ref, select_ref, group_ref, out_ref, rows):
    for j in range(5):
        out_ref[j] = packed_group(j, sum_ref, select_ref, group_ref, rows)


def pack_low_kernel(sum_ref, select_ref, group_ref, part_ref, sent_ref, out_ref, rows):
    for j in range(5):
        found = part_ref[j] + packed_group(j, sum_ref, select_ref, group_ref, rows)
        for k in range(GROUP):
            out_ref[pl.ds(j * GROUP + k, 128, stride=CHUNK), :] = found[k * 128 : (k + 1) * 128]
    out_ref[pl.ds(CAP + GROUP, 128, stride=CHUNK), :] = sent_ref[...]


def update_kernel(
    got_ref, table_ref, sums_ref, b0, b1, b2, b3, new_table_ref, new_sum_ref, wk_grad, wv_grad, values, select
):
    width = wk_grad.shape[1]
    total = (b0[...] + b1[...]) + (b2[...] + b3[...])
    wk_grad[...] = total[:, :width]
    wv_grad[...] = total[:, width:]
    owned = table_ref.shape[1]
    slots = got_ref[pl.ds(CAP + GROUP, 128, stride=CHUNK), :]
    ids = (lax.broadcasted_iota(jnp.int32, (128, owned), 1) + 1).astype(F32)
    for k in range(CAP):
        at = slice(k * 128, (k + 1) * 128)
        select[at, :] = jnp.where(slots[:, k : k + 1] == ids, 1.0, 0.0).astype(BF16)
        main = got_ref[pl.ds(k, 128, stride=CHUNK), :].T
        top = main.astype(BF16)
        values[:MAIN, at] = top
        values[EH : EH + MAIN, at] = (main - top.astype(F32)).astype(BF16)
    for k in range(GROUP):
        tail = got_ref[pl.ds(CAP + k, 128, stride=CHUNK), :].T
        top = tail.astype(BF16)
        rest = (tail - top.astype(F32)).astype(BF16)
        for j in range(4):
            at = slice((j * GROUP + k) * 128, (j * GROUP + k + 1) * 128)
            values[MAIN:EH, at] = top[j * TAIL : (j + 1) * TAIL]
            values[EH + MAIN :, at] = rest[j * TAIL : (j + 1) * TAIL]
    both = jnp.dot(values[...], select[...], preferred_element_type=F32)
    row_sum = both[:EH] + both[EH:]
    new_sum = sums_ref[...] + row_sum * row_sum
    new_sum_ref[...] = new_sum
    new_table_ref[...] = table_ref[...] - LEARN_RATE * row_sum / (jnp.sqrt(new_sum) + EPSILON)


def whole(shape):
    return pl.BlockSpec(shape, lambda *_: (0,) * len(shape))


def body(hidden, out_grad, memory, w_key, w_value, row_owner, row_slot, mem_table, adagrad_sum):
    tokens, width = hidden.shape
    depth = memory.shape[1]
    quarter = tokens // 4
    tile = 256
    tiles = tokens // tile

    position = lax.axis_index("dp").astype(jnp.int32)
    core = position & 1
    place = jnp.stack([position >> 3, (position >> 1) & 3, core])
    at = jnp.stack([lax.axis_index("tensor").astype(jnp.int32), core])

    def quarter_at(p, s):
        return (s[0] + 4 + (1 + p) * (2 * s[1] - 1)) & 3

    start = quarter_at(0, at).reshape(1)

    def by_rows(cols):
        return pl.BlockSpec((tile, cols), lambda i, s: (i, 0))

    chunk = whole((quarter, 2 * width))
    part, first_both = pl.pallas_call(
        forward_kernel,
        grid_spec=pltpu.PrefetchScalarGridSpec(
            num_scalar_prefetch=1,
            grid=(tiles,),
            in_specs=[
                by_rows(depth),
                by_rows(width),
                by_rows(width),
                whole((depth, width)),
                whole((depth, width)),
            ],
            out_specs=[
                pl.BlockSpec((2, tile), lambda i, s: (0, i)),
                chunk,
            ],
        ),
        out_shape=[
            jax.ShapeDtypeStruct((2, tokens), F32),
            jax.ShapeDtypeStruct((quarter, 2 * width), BF16),
        ],
        compiler_params=params(53),
        cost_estimate=cost(4 * tokens * depth * width, 12 << 20),
        name="forward",
    )(start, memory, hidden, out_grad, w_key, w_value)
    parts = [part] + [
        lax.ppermute(part, "tensor", [(i, (i + step) % 4) for i in range(4)]) for step in (1, 2, 3)
    ]

    def swapped(value, bits):
        def goal(i):
            dp, tensor = i // 4, i % 4
            by = bits[dp % 2]
            return (dp ^ by[0]) * 4 + (tensor ^ by[1])

        return lax.ppermute(value, ("dp", "tensor"), [(i, goal(i)) for i in range(128)])

    def turned(value):
        def goal(i):
            return i // 4 * 4 + (i + (1, 3)[i // 4 % 2]) % 4

        return lax.ppermute(value, ("dp", "tensor"), [(i, goal(i)) for i in range(128)])

    def tile_spec(cols):
        return pl.BlockSpec((quarter, cols), lambda p, s: (quarter_at(p, s), 0))

    weights = [whole((depth, width))] * 2
    part_whole = whole((2, tokens))
    top = 128
    low = quarter - top

    first_top, first_low = pl.pallas_call(
        first_kernel,
        grid_spec=pltpu.PrefetchScalarGridSpec(
            num_scalar_prefetch=1,
            grid=(1,),
            in_specs=[part_whole] * 4 + [chunk] + weights,
            out_specs=[whole((top, depth)), whole((low, depth))],
        ),
        out_shape=[
            jax.ShapeDtypeStruct((top, depth), F32),
            jax.ShapeDtypeStruct((low, depth), F32),
        ],
        compiler_params=params(20),
        cost_estimate=cost(4 * quarter * depth * width, 6 << 20),
        name="first",
    )(start, *parts, first_both, w_key, w_value)
    parts, _ = lax.optimization_barrier((parts, first_low))

    def by_rows(cols):
        return pl.BlockSpec((quarter, cols), lambda i: (i, 0))

    total_spec = pl.BlockSpec((2, quarter), lambda i: (0, i))
    both = pl.pallas_call(
        gate_kernel,
        grid=(4,),
        in_specs=[total_spec] * 4 + [by_rows(width)] * 2,
        out_specs=by_rows(2 * width),
        out_shape=jax.ShapeDtypeStruct((tokens, 2 * width), BF16),
        compiler_params=params(24),
        cost_estimate=cost(1, 1),
        name="gate",
    )(*parts, hidden, out_grad)

    grad_spec = whole((depth // 2, 2 * width))
    mine, other = pl.pallas_call(
        weight_grad_kernel,
        grid_spec=pltpu.PrefetchScalarGridSpec(
            num_scalar_prefetch=1,
            grid=(2,),
            in_specs=[
                pl.BlockSpec((tokens, depth // 2), lambda i, s: (0, i)),
                whole((tokens, 2 * width)),
            ],
            out_specs=[grad_spec, grad_spec],
        ),
        out_shape=[jax.ShapeDtypeStruct((depth // 2, 2 * width), F32)] * 2,
        compiler_params=params(32),
        cost_estimate=cost(1, 1),
        name="weight_grad",
    )(place, memory, both)
    late, _ = lax.optimization_barrier((both, other))
    rest_top, rest_low = pl.pallas_call(
        rest_kernel,
        grid_spec=pltpu.PrefetchScalarGridSpec(
            num_scalar_prefetch=1,
            grid=(3,),
            in_specs=[
                pl.BlockSpec((quarter, 2 * width), lambda p, s: (quarter_at(p + 1, s), 0)),
                *weights,
            ],
            out_specs=[
                pl.BlockSpec((1, top, depth), lambda p, s: (p, 0, 0)),
                pl.BlockSpec((1, low, depth), lambda p, s: (p, 0, 0)),
            ],
        ),
        out_shape=[
            jax.ShapeDtypeStruct((3, top, depth), F32),
            jax.ShapeDtypeStruct((3, low, depth), F32),
        ],
        compiler_params=params(24),
        cost_estimate=cost(1, 1),
        name="rest",
    )(at, late, w_key, w_value)

    def folded(value, bits):
        half = value.shape[0] // 2
        return value[:half] + swapped(value[half:], bits)

    moved_top = turned(first_top) + rest_top[0]
    moved_low = turned(first_low) + rest_low[0]
    moved_top, moved_low, owners, slots = lax.optimization_barrier(
        (moved_top, moved_low, row_owner.T, row_slot.T)
    )
    passed_top = turned(moved_top)
    passed_low = turned(moved_low)
    select, group, sent = pl.pallas_call(
        ranks_kernel,
        grid_spec=pltpu.PrefetchScalarGridSpec(
            num_scalar_prefetch=1,
            grid=(1,),
            in_specs=[pl.BlockSpec((HEADS, quarter), lambda i, s: (0, s[0]))] * 2,
            out_specs=[
                whole((GROUP * 128, HEADS * quarter)),
                whole((HEADS * quarter, 128)),
                whole((128, 128)),
            ],
        ),
        out_shape=[
            jax.ShapeDtypeStruct((GROUP * 128, HEADS * quarter), BF16),
            jax.ShapeDtypeStruct((HEADS * quarter, 128), F32),
            jax.ShapeDtypeStruct((128, 128), F32),
        ],
        compiler_params=params(32),
        cost_estimate=cost(1 << 36, 1 << 27),
        name="ranks",
    )(at, owners, slots)
    mine, select = lax.optimization_barrier((mine, select))
    pair = mine + swapped(other, ((1, 0), (1, 0)))
    rest_top, rest_low, pair = lax.optimization_barrier((rest_top, rest_low, pair))
    moved_top = turned(passed_top + rest_top[1])
    moved_low = turned(passed_low + rest_low[1])
    grads = folded(pair, ((8, 0), (2, 0)))
    rest_top, rest_low, grads = lax.optimization_barrier((rest_top, rest_low, grads))
    sum_top = moved_top + rest_top[2]
    sum_low = moved_low + rest_low[2]
    grads = folded(grads, ((24, 0), (6, 0)))

    half_rows = HEADS * quarter // 2

    def piece_specs(piece):
        return [
            whole((quarter // 2, depth)),
            pl.BlockSpec((GROUP * 128, half_rows), lambda i: (0, piece)),
            pl.BlockSpec((half_rows, 128), lambda i: (piece, 0)),
        ]

    pack_part = pl.pallas_call(
        pack_top_kernel,
        grid=(1,),
        in_specs=piece_specs(0),
        out_specs=whole((5, GROUP * 128, 128)),
        out_shape=jax.ShapeDtypeStruct((5, GROUP * 128, 128), F32),
        scratch_shapes=[pltpu.VMEM((5, half_rows, 256), BF16)],
        compiler_params=params(24),
        cost_estimate=cost(1024 * 2048 * 1280, 8 << 20),
        name="pack_top",
    )(sum_top, select, group)
    packed = pl.pallas_call(
        pack_low_kernel,
        grid=(1,),
        in_specs=[
            *piece_specs(1),
            whole((5, GROUP * 128, 128)),
            whole((128, 128)),
        ],
        out_specs=whole((128 * CHUNK, 128)),
        out_shape=jax.ShapeDtypeStruct((128 * CHUNK, 128), F32),
        scratch_shapes=[pltpu.VMEM((5, half_rows, 256), BF16)],
        compiler_params=params(32),
        cost_estimate=cost(1024 * 2048 * 1280, 12 << 20),
        name="pack_low",
    )(sum_low, select, group, pack_part, sent)
    packed, grads, parts = lax.optimization_barrier((packed, grads, parts))
    hidden_grad = pl.pallas_call(
        hidden_grad_kernel,
        grid=(4,),
        in_specs=[total_spec] * 4 + [by_rows(depth), whole((depth, width))],
        out_specs=by_rows(width),
        out_shape=jax.ShapeDtypeStruct((tokens, width), BF16),
        compiler_params=params(58),
        cost_estimate=cost(2 * tokens * depth * width, 6 << 20),
        name="hidden_grad",
    )(*parts, memory, w_key)
    received = lax.all_to_all(
        packed.reshape(128, 1, CHUNK * 128),
        ("dp", "tensor"),
        split_axis=0,
        concat_axis=0,
        tiled=True,
    ).reshape(128 * CHUNK, 128)
    blocks = grads.reshape(4, -1, 2 * width)
    got = [
        swapped(blocks[i], ((2 * bits, 0), (8 * bits, 0))) for i, bits in ((1, 3), (2, 1), (3, 2))
    ]
    received, hidden_grad = lax.optimization_barrier((received, hidden_grad))
    owned = mem_table.shape[0]
    share = blocks.shape[1]
    table_spec = whole((EH, owned))
    new_table, new_sum, key_weight_grad, value_weight_grad = pl.pallas_call(
        update_kernel,
        grid=(1,),
        in_specs=[whole((128 * CHUNK, 128)), table_spec, table_spec]
        + [whole((share, 2 * width))] * 4,
        out_specs=[table_spec, table_spec] + [whole((share, width))] * 2,
        out_shape=[jax.ShapeDtypeStruct((EH, owned), F32)] * 2
        + [jax.ShapeDtypeStruct((share, width), F32)] * 2,
        scratch_shapes=[
            pltpu.VMEM((2 * EH, CAP * 128), BF16),
            pltpu.VMEM((CAP * 128, owned), BF16),
        ],
        compiler_params=params(48),
        cost_estimate=cost(4 * EH * 4096 * 512, 5 << 20),
        name="update",
    )(received, mem_table.T, adagrad_sum.T, blocks[0], *got)
    return (hidden_grad, key_weight_grad, value_weight_grad, new_table.T, new_sum.T)


def solution(mesh):
    return jax.shard_map(
        body,
        mesh=mesh,
        in_specs=(
            P("dp", "tensor"),
            P("dp", "tensor"),
            P("dp", None),
            P(None, "tensor"),
            P(None, "tensor"),
            P("dp", None),
            P("dp", None),
            P(("dp", "tensor"), None),
            P(("dp", "tensor"), None),
        ),
        out_specs=(
            P("dp", "tensor"),
            P("dp", "tensor"),
            P("dp", "tensor"),
            P(("dp", "tensor"), None),
            P(("dp", "tensor"), None),
        ),
        check_vma=False,
    )
```

```python
import functools

import jax
import jax.numpy as jnp
from jax import lax
from jax.experimental import pallas as pl
from jax.experimental.pallas import tpu as pltpu
from jax.sharding import PartitionSpec as P

D = 2560
HEADS = 8
EH = 160
MAIN = 128
TAIL = EH - MAIN
CAP = 32
GROUP = CAP // 4
CHUNK = CAP + GROUP + 1
LEARN_RATE = 0.5
EPSILON = 1e-06
F32 = jnp.float32
BF16 = jnp.bfloat16
OVER_ROWS = (((0,), (0,)), ((), ()))
OVER_LANES = (((1,), (1,)), ((), ()))


def params(mib):
    return pltpu.CompilerParams(vmem_limit_bytes=mib << 20)


def cost(flops, moved):
    return pl.CostEstimate(flops=flops, bytes_accessed=moved, transcendentals=0)


def row_sums(x):
    lanes = x[:, :128]
    for at in range(128, x.shape[1], 128):
        lanes = lanes + x[:, at : at + 128]
    return jnp.sum(lanes.T, axis=0, keepdims=True)


def as_columns(row, width):
    column = jnp.broadcast_to(row, (128, row.shape[1])).T
    return jnp.concatenate([column] * (width // 128), axis=1)


def ranks_kernel(at_ref, owners_ref, slots_ref, select_ref, group_ref, sent_ref):
    count = owners_ref.shape[1]
    owners = owners_ref[...]
    slot_plus = slots_ref[...] + 1
    ids = lax.broadcasted_iota(jnp.int32, (128, count), 0)
    hits = jnp.zeros((128, count), F32)
    for h in range(HEADS):
        hits = hits + jnp.where(owners[h : h + 1] == ids, 1.0, 0.0)
    earlier = lax.broadcasted_iota(jnp.int32, (count, count), 0) < lax.broadcasted_iota(
        jnp.int32, (count, count), 1
    )
    before = jnp.dot(
        hits.astype(BF16), jnp.where(earlier, 1.0, 0.0).astype(BF16), preferred_element_type=F32
    )
    high = jnp.zeros((128, 128), F32)
    low = jnp.zeros((128, 128), F32)
    for h in range(HEADS):
        match = owners[h : h + 1] == ids
        rank = jnp.sum(jnp.where(match, before, 0.0), axis=0, keepdims=True).astype(jnp.int32)
        place = jnp.where(rank == ids, 1.0, 0.0).astype(BF16)
        slot = slot_plus[h : h + 1]
        upper = jnp.where(match, (slot // 16).astype(F32), 0.0).astype(BF16)
        lower = jnp.where(match, (slot % 16).astype(F32), 0.0).astype(BF16)
        high = high + lax.dot_general(upper, place, OVER_LANES, preferred_element_type=F32)
        low = low + lax.dot_general(lower, place, OVER_LANES, preferred_element_type=F32)
        groups = jnp.broadcast_to((rank // GROUP).astype(F32), (128, count)).T
        within = jnp.where(match, rank % GROUP, -1)
        for piece in range(2):
            tokens = slice(piece * 128, (piece + 1) * 128)
            columns = slice((piece * HEADS + h) * 128, (piece * HEADS + h + 1) * 128)
            group_ref[columns, :] = groups[tokens]
            for k in range(GROUP):
                select_ref[k * 128 : (k + 1) * 128, columns] = jnp.where(
                    within[:, tokens] == k, 1.0, 0.0
                ).astype(BF16)
    sent_ref[...] = 16.0 * high + low


def forward_kernel(
    at_ref, memory_ref, hidden_ref, grad_ref, wk_ref, wv_ref, part_ref, first_ref
):
    @pl.when(pl.program_id(0) == at_ref[0])
    def _():
        width = hidden_ref.shape[1]
        first_ref[:, :width] = hidden_ref[...]
        first_ref[:, width:] = grad_ref[...]

    memory = memory_ref[...]
    proj_key = jnp.dot(memory, wk_ref[...], preferred_element_type=F32)
    part_ref[0:1, :] = row_sums(hidden_ref[...].astype(F32) * proj_key)
    proj_value = jnp.dot(memory, wv_ref[...], preferred_element_type=F32)
    part_ref[1:2, :] = row_sums(grad_ref[...].astype(F32) * proj_value)


def gate_columns(total, width):
    root = jnp.sqrt(jnp.full((1, 1), D, F32))
    gate = jax.nn.sigmoid(total[0:1] / root)
    score = total[1:2] * gate * (1.0 - gate) / root
    return as_columns(gate, width), as_columns(score, width)


def summed_parts(part_refs, at=slice(None)):
    p0, p1, p2, p3 = (ref[:, at] for ref in part_refs)
    return (p0 + p1) + (p2 + p3)


def memory_grad_tile(key_grad, value_grad, wk_ref, wv_ref, *out_refs):
    grads = lax.dot_general(
        key_grad, wk_ref[...], OVER_LANES, preferred_element_type=F32
    ) + lax.dot_general(value_grad, wv_ref[...], OVER_LANES, preferred_element_type=F32)
    at = 0
    for out_ref in out_refs:
        here = grads[at : at + out_ref.shape[0]]
        for h in range(HEADS):
            first = h * EH
            out_ref[:, h * MAIN : (h + 1) * MAIN] = here[:, first : first + MAIN]
            tail = slice(HEADS * MAIN + h * TAIL, HEADS * MAIN + (h + 1) * TAIL)
            out_ref[:, tail] = here[:, first + MAIN : first + EH]
        at += out_ref.shape[0]


def first_kernel(at_ref, p0, p1, p2, p3, first_ref, wk_ref, wv_ref, out_ref):
    count, width = first_ref.shape[0], first_ref.shape[1] // 2
    tile = pl.ds(pl.multiple_of(at_ref[0] * count, count), count)
    gates, scores = gate_columns(summed_parts((p0, p1, p2, p3), tile), width)
    key_grad = (scores * first_ref[:, :width].astype(F32)).astype(BF16)
    value_grad = (gates * first_ref[:, width:].astype(F32)).astype(BF16)
    memory_grad_tile(key_grad, value_grad, wk_ref, wv_ref, out_ref)


def gate_kernel(p0, p1, p2, p3, hidden_ref, grad_ref, both_ref):
    width = hidden_ref.shape[1]
    gates, scores = gate_columns(summed_parts((p0, p1, p2, p3)), width)
    both_ref[:, :width] = (scores * hidden_ref[...].astype(F32)).astype(BF16)
    both_ref[:, width:] = (gates * grad_ref[...].astype(F32)).astype(BF16)


def hidden_grad_kernel(p0, p1, p2, p3, memory_ref, wk_ref, out_ref):
    _, scores = gate_columns(summed_parts((p0, p1, p2, p3)), out_ref.shape[1])
    proj_key = jnp.dot(memory_ref[...], wk_ref[...], preferred_element_type=F32)
    out_ref[...] = (scores * proj_key).astype(BF16)


def rest_kernel(at_ref, both_ref, wk_ref, wv_ref, top_ref, low_ref):
    width = wk_ref.shape[1]
    memory_grad_tile(
        both_ref[:, :width], both_ref[:, width:], wk_ref, wv_ref, top_ref.at[0], low_ref.at[0]
    )


def weight_grad_kernel(at_ref, memory_ref, both_ref, mine_ref, other_ref):
    i = pl.program_id(0)
    block = mine_ref.shape[0] // 16
    rows = memory_ref.shape[1]
    me_x, me_z, me_core = at_ref[0], at_ref[1], at_ref[2]

    def order(r):
        return jnp.where(r == 0, 0, jnp.where(r == 3, 1, r + 1))

    found = lax.dot_general(
        memory_ref[...], both_ref[...], OVER_ROWS, preferred_element_type=F32
    )
    for p in range(rows // block):
        x = order((i * 2 + p // 8) ^ me_x)
        z = order((p % 8 // 2) ^ me_z)
        place = x * 4 + z if p % 2 == 0 else z * 4 + x
        to = pl.ds(pl.multiple_of(place * block, 8), block)
        value = found[p * block : (p + 1) * block]

        @pl.when(me_core == p % 2)
        def _():
            mine_ref[to, :] = value

        @pl.when(me_core != p % 2)
        def _():
            other_ref[to, :] = value


def packed_group(j, sum_ref, select_ref, group_ref, rows):
    count = sum_ref.shape[0]
    lane_group = lax.broadcasted_iota(jnp.int32, (count, 128), 1) // TAIL
    for h in range(HEADS):
        group = group_ref[h * count : (h + 1) * count, :]
        if j < 4:
            value = jnp.where(group == j, sum_ref[:, h * MAIN : (h + 1) * MAIN], 0.0)
        else:
            at = HEADS * MAIN + h * TAIL
            tail = jnp.concatenate([sum_ref[:, at : at + TAIL]] * 4, axis=1)
            value = jnp.where(group == lane_group.astype(F32), tail, 0.0)
        top = value.astype(BF16)
        rows[j, h * count : (h + 1) * count, :MAIN] = top
        rows[j, h * count : (h + 1) * count, MAIN:] = (value - top.astype(F32)).astype(BF16)
    found = jnp.dot(select_ref[...], rows[j], preferred_element_type=F32)
    return found[:, :MAIN] + found[:, MAIN:]


def pack_top_kernel(sum_ref, select_ref, group_ref, out_ref, rows):
    for j in range(5):
        out_ref[j] = packed_group(j, sum_ref, select_ref, group_ref, rows)


def pack_low_kernel(sum_ref, select_ref, group_ref, part_ref, sent_ref, out_ref, rows):
    for j in range(5):
        found = part_ref[j] + packed_group(j, sum_ref, select_ref, group_ref, rows)
        for k in range(GROUP):
            out_ref[pl.ds(j * GROUP + k, 128, stride=CHUNK), :] = found[k * 128 : (k + 1) * 128]
    out_ref[pl.ds(CAP + GROUP, 128, stride=CHUNK), :] = sent_ref[...]


def update_kernel(
    got_ref, table_ref, sums_ref, b0, b1, b2, b3, new_table_ref, new_sum_ref, wk_grad, wv_grad, values, select
):
    width = wk_grad.shape[1]
    total = (b0[...] + b1[...]) + (b2[...] + b3[...])
    wk_grad[...] = total[:, :width]
    wv_grad[...] = total[:, width:]
    owned = table_ref.shape[1]
    slots = got_ref[pl.ds(CAP + GROUP, 128, stride=CHUNK), :]
    ids = (lax.broadcasted_iota(jnp.int32, (128, owned), 1) + 1).astype(F32)
    for k in range(CAP):
        at = slice(k * 128, (k + 1) * 128)
        select[at, :] = jnp.where(slots[:, k : k + 1] == ids, 1.0, 0.0).astype(BF16)
        main = got_ref[pl.ds(k, 128, stride=CHUNK), :].T
        top = main.astype(BF16)
        values[:MAIN, at] = top
        values[EH : EH + MAIN, at] = (main - top.astype(F32)).astype(BF16)
    for k in range(GROUP):
        tail = got_ref[pl.ds(CAP + k, 128, stride=CHUNK), :].T
        top = tail.astype(BF16)
        rest = (tail - top.astype(F32)).astype(BF16)
        for j in range(4):
            at = slice((j * GROUP + k) * 128, (j * GROUP + k + 1) * 128)
            values[MAIN:EH, at] = top[j * TAIL : (j + 1) * TAIL]
            values[EH + MAIN :, at] = rest[j * TAIL : (j + 1) * TAIL]
    both = jnp.dot(values[...], select[...], preferred_element_type=F32)
    row_sum = both[:EH] + both[EH:]
    new_sum = sums_ref[...] + row_sum * row_sum
    new_sum_ref[...] = new_sum
    new_table_ref[...] = table_ref[...] - LEARN_RATE * row_sum / (jnp.sqrt(new_sum) + EPSILON)


def whole(shape):
    return pl.BlockSpec(shape, lambda *_: (0,) * len(shape))


def body(hidden, out_grad, memory, w_key, w_value, row_owner, row_slot, mem_table, adagrad_sum):
    tokens, width = hidden.shape
    depth = memory.shape[1]
    quarter = tokens // 4
    tile = 256
    tiles = tokens // tile

    position = lax.axis_index("dp").astype(jnp.int32)
    core = position & 1
    place = jnp.stack([position >> 3, (position >> 1) & 3, core])
    at = jnp.stack([lax.axis_index("tensor").astype(jnp.int32), core])

    def quarter_at(p, s):
        return (s[0] + 4 + (1 + p) * (2 * s[1] - 1)) & 3

    start = quarter_at(0, at).reshape(1)

    def by_rows(cols):
        return pl.BlockSpec((tile, cols), lambda i, s: (i, 0))

    chunk = whole((quarter, 2 * width))
    part, first_both = pl.pallas_call(
        forward_kernel,
        grid_spec=pltpu.PrefetchScalarGridSpec(
            num_scalar_prefetch=1,
            grid=(tiles,),
            in_specs=[
                by_rows(depth),
                by_rows(width),
                by_rows(width),
                whole((depth, width)),
                whole((depth, width)),
            ],
            out_specs=[
                pl.BlockSpec((2, tile), lambda i, s: (0, i)),
                chunk,
            ],
        ),
        out_shape=[
            jax.ShapeDtypeStruct((2, tokens), F32),
            jax.ShapeDtypeStruct((quarter, 2 * width), BF16),
        ],
        compiler_params=params(53),
        cost_estimate=cost(4 * tokens * depth * width, 12 << 20),
        name="forward",
    )(start, memory, hidden, out_grad, w_key, w_value)
    parts = [part] + [
        lax.ppermute(part, "tensor", [(i, (i + step) % 4) for i in range(4)]) for step in (1, 2, 3)
    ]

    def swapped(value, bits):
        def goal(i):
            dp, tensor = i // 4, i % 4
            by = bits[dp % 2]
            return (dp ^ by[0]) * 4 + (tensor ^ by[1])

        return lax.ppermute(value, ("dp", "tensor"), [(i, goal(i)) for i in range(128)])

    def turned(value):
        def goal(i):
            return i // 4 * 4 + (i + (1, 3)[i // 4 % 2]) % 4

        return lax.ppermute(value, ("dp", "tensor"), [(i, goal(i)) for i in range(128)])

    def tile_spec(cols):
        return pl.BlockSpec((quarter, cols), lambda p, s: (quarter_at(p, s), 0))

    weights = [whole((depth, width))] * 2
    part_whole = whole((2, tokens))
    top = 128
    low = quarter - top

    first = pl.pallas_call(
        first_kernel,
        grid_spec=pltpu.PrefetchScalarGridSpec(
            num_scalar_prefetch=1,
            grid=(1,),
            in_specs=[part_whole] * 4 + [chunk] + weights,
            out_specs=whole((quarter, depth)),
        ),
        out_shape=jax.ShapeDtypeStruct((quarter, depth), F32),
        compiler_params=params(20),
        cost_estimate=cost(4 * quarter * depth * width, 6 << 20),
        name="first",
    )(start, *parts, first_both, w_key, w_value)
    parts, _ = lax.optimization_barrier((parts, first))

    def by_rows(cols):
        return pl.BlockSpec((quarter, cols), lambda i: (i, 0))

    total_spec = pl.BlockSpec((2, quarter), lambda i: (0, i))
    both = pl.pallas_call(
        gate_kernel,
        grid=(4,),
        in_specs=[total_spec] * 4 + [by_rows(width)] * 2,
        out_specs=by_rows(2 * width),
        out_shape=jax.ShapeDtypeStruct((tokens, 2 * width), BF16),
        compiler_params=params(24),
        cost_estimate=cost(1, 1),
        name="gate",
    )(*parts, hidden, out_grad)

    grad_spec = whole((depth // 2, 2 * width))
    mine, other = pl.pallas_call(
        weight_grad_kernel,
        grid_spec=pltpu.PrefetchScalarGridSpec(
            num_scalar_prefetch=1,
            grid=(2,),
            in_specs=[
                pl.BlockSpec((tokens, depth // 2), lambda i, s: (0, i)),
                whole((tokens, 2 * width)),
            ],
            out_specs=[grad_spec, grad_spec],
        ),
        out_shape=[jax.ShapeDtypeStruct((depth // 2, 2 * width), F32)] * 2,
        compiler_params=params(32),
        cost_estimate=cost(1, 1),
        name="weight_grad",
    )(place, memory, both)
    late, _ = lax.optimization_barrier((both, other))
    rest_top, rest_low = pl.pallas_call(
        rest_kernel,
        grid_spec=pltpu.PrefetchScalarGridSpec(
            num_scalar_prefetch=1,
            grid=(3,),
            in_specs=[
                pl.BlockSpec((quarter, 2 * width), lambda p, s: (quarter_at(p + 1, s), 0)),
                *weights,
            ],
            out_specs=[
                pl.BlockSpec((1, top, depth), lambda p, s: (p, 0, 0)),
                pl.BlockSpec((1, low, depth), lambda p, s: (p, 0, 0)),
            ],
        ),
        out_shape=[
            jax.ShapeDtypeStruct((3, top, depth), F32),
            jax.ShapeDtypeStruct((3, low, depth), F32),
        ],
        compiler_params=params(24),
        cost_estimate=cost(1, 1),
        name="rest",
    )(at, late, w_key, w_value)

    def folded(value, bits):
        half = value.shape[0] // 2
        return value[:half] + swapped(value[half:], bits)

    moved_top = turned(first[:top]) + rest_top[0]
    moved_low = turned(first[top:]) + rest_low[0]
    moved_top, moved_low, owners, slots = lax.optimization_barrier(
        (moved_top, moved_low, row_owner.T, row_slot.T)
    )
    passed_top = turned(moved_top)
    passed_low = turned(moved_low)
    select, group, sent = pl.pallas_call(
        ranks_kernel,
        grid_spec=pltpu.PrefetchScalarGridSpec(
            num_scalar_prefetch=1,
            grid=(1,),
            in_specs=[pl.BlockSpec((HEADS, quarter), lambda i, s: (0, s[0]))] * 2,
            out_specs=[
                whole((GROUP * 128, HEADS * quarter)),
                whole((HEADS * quarter, 128)),
                whole((128, 128)),
            ],
        ),
        out_shape=[
            jax.ShapeDtypeStruct((GROUP * 128, HEADS * quarter), BF16),
            jax.ShapeDtypeStruct((HEADS * quarter, 128), F32),
            jax.ShapeDtypeStruct((128, 128), F32),
        ],
        compiler_params=params(32),
        cost_estimate=cost(1 << 36, 1 << 27),
        name="ranks",
    )(at, owners, slots)
    mine, select = lax.optimization_barrier((mine, select))
    pair = mine + swapped(other, ((1, 0), (1, 0)))
    rest_top, rest_low, pair = lax.optimization_barrier((rest_top, rest_low, pair))
    moved_top = turned(passed_top + rest_top[1])
    moved_low = turned(passed_low + rest_low[1])
    grads = folded(pair, ((8, 0), (2, 0)))
    rest_top, rest_low, grads = lax.optimization_barrier((rest_top, rest_low, grads))
    sum_top = moved_top + rest_top[2]
    sum_low = moved_low + rest_low[2]
    grads = folded(grads, ((24, 0), (6, 0)))

    half_rows = HEADS * quarter // 2

    def piece_specs(piece):
        return [
            whole((quarter // 2, depth)),
            pl.BlockSpec((GROUP * 128, half_rows), lambda i: (0, piece)),
            pl.BlockSpec((half_rows, 128), lambda i: (piece, 0)),
        ]

    pack_part = pl.pallas_call(
        pack_top_kernel,
        grid=(1,),
        in_specs=piece_specs(0),
        out_specs=whole((5, GROUP * 128, 128)),
        out_shape=jax.ShapeDtypeStruct((5, GROUP * 128, 128), F32),
        scratch_shapes=[pltpu.VMEM((5, half_rows, 256), BF16)],
        compiler_params=params(24),
        cost_estimate=cost(1024 * 2048 * 1280, 8 << 20),
        name="pack_top",
    )(sum_top, select, group)
    packed = pl.pallas_call(
        pack_low_kernel,
        grid=(1,),
        in_specs=[
            *piece_specs(1),
            whole((5, GROUP * 128, 128)),
            whole((128, 128)),
        ],
        out_specs=whole((128 * CHUNK, 128)),
        out_shape=jax.ShapeDtypeStruct((128 * CHUNK, 128), F32),
        scratch_shapes=[pltpu.VMEM((5, half_rows, 256), BF16)],
        compiler_params=params(32),
        cost_estimate=cost(1024 * 2048 * 1280, 12 << 20),
        name="pack_low",
    )(sum_low, select, group, pack_part, sent)
    packed, grads, parts = lax.optimization_barrier((packed, grads, parts))
    hidden_grad = pl.pallas_call(
        hidden_grad_kernel,
        grid=(4,),
        in_specs=[total_spec] * 4 + [by_rows(depth), whole((depth, width))],
        out_specs=by_rows(width),
        out_shape=jax.ShapeDtypeStruct((tokens, width), BF16),
        compiler_params=params(58),
        cost_estimate=cost(2 * tokens * depth * width, 6 << 20),
        name="hidden_grad",
    )(*parts, memory, w_key)
    received = lax.all_to_all(
        packed.reshape(128, 1, CHUNK * 128),
        ("dp", "tensor"),
        split_axis=0,
        concat_axis=0,
        tiled=True,
    ).reshape(128 * CHUNK, 128)
    blocks = grads.reshape(4, -1, 2 * width)
    got = [
        swapped(blocks[i], ((2 * bits, 0), (8 * bits, 0))) for i, bits in ((1, 3), (2, 1), (3, 2))
    ]
    received, hidden_grad = lax.optimization_barrier((received, hidden_grad))
    owned = mem_table.shape[0]
    share = blocks.shape[1]
    table_spec = whole((EH, owned))
    new_table, new_sum, key_weight_grad, value_weight_grad = pl.pallas_call(
        update_kernel,
        grid=(1,),
        in_specs=[whole((128 * CHUNK, 128)), table_spec, table_spec]
        + [whole((share, 2 * width))] * 4,
        out_specs=[table_spec, table_spec] + [whole((share, width))] * 2,
        out_shape=[jax.ShapeDtypeStruct((EH, owned), F32)] * 2
        + [jax.ShapeDtypeStruct((share, width), F32)] * 2,
        scratch_shapes=[
            pltpu.VMEM((2 * EH, CAP * 128), BF16),
            pltpu.VMEM((CAP * 128, owned), BF16),
        ],
        compiler_params=params(48),
        cost_estimate=cost(4 * EH * 4096 * 512, 5 << 20),
        name="update",
    )(received, mem_table.T, adagrad_sum.T, blocks[0], *got)
    return (hidden_grad, key_weight_grad, value_weight_grad, new_table.T, new_sum.T)


def solution(mesh):
    return jax.shard_map(
        body,
        mesh=mesh,
        in_specs=(
            P("dp", "tensor"),
            P("dp", "tensor"),
            P("dp", None),
            P(None, "tensor"),
            P(None, "tensor"),
            P("dp", None),
            P("dp", None),
            P(("dp", "tensor"), None),
            P(("dp", "tensor"), None),
        ),
        out_specs=(
            P("dp", "tensor"),
            P("dp", "tensor"),
            P("dp", "tensor"),
            P(("dp", "tensor"), None),
            P(("dp", "tensor"), None),
        ),
        check_vma=False,
    )
```
